512 devices in a mesh: ctx: 64 (over z_hi, x, y), head: 8 (over z_lo, core).
Axes of the slice: x: 4, y: 4, z: 16 (z_hi: 4, z_lo: 4; z = z_hi * 4 + z_lo), core: 2. Of those that a mesh axis runs over, the one named last changes fastest.
Arguments:
- queries: bfloat16 [16384, 6144], P(('ctx', 'head')), may hold values from -32 to 32
- keys: bfloat16 [16384, 6144], P(('ctx', 'head')), may hold values from -12 to 12
- values: bfloat16 [16384, 6144], P(('ctx', 'head')), may hold values from -6 to 6
- cache_keys: bfloat16 [32768, 6144], P('ctx', 'head'), may hold values from -6 to 6
- cache_values: bfloat16 [32768, 6144], P('ctx', 'head'), may hold values from -6 to 6
- pattern: int32 [128, 4], replicated, may hold values from 0 to 255, as said below
- reached: int32 [128], replicated, may hold values from 1 to 4, as said below
- gate: float32 [6144], replicated, may hold values from 0.5 to 2
Outputs:
- mixed: bfloat16 [16384, 6144], P(('ctx', 'head'))
The draws below stay inside these ranges and needn't reach their ends.
Inputs may be any that keep to these rules, and one draw needn't show every extreme that they name: `pattern`: every entry of row g names a cached tile of ctx index g // 2 - 1, g // 2 or g // 2 + 1, where ctx index c holds cached tiles c * 4 to (c + 1) * 4 - 1. Only the first reached[g] entries of row g of pattern are used.
All inputs are finite; a program needn't handle non-finite values.
Results may differ from the reference program's by a relative error of at most 0.011.
Values may be sent and summed in bfloat16 or wider, within the bound.
No kernel may reach another device: no remote copies, remote signals or barrier semaphores. Data moves between devices by JAX's collectives and lax.ppermute only.
A program may use at most 64 MiB of HBM per device.

```python
import jax
import jax.numpy as jnp
from jax import lax

D = 6144
HEADS = 48
HD = 128
TILE = 128
REACH = 4
CT_DEV = 4
QT_DEV = 2
QTILES = 128
CTILES = 256
TOKENS = 16384
N_CTX = 64


def query_key_pair(key):
    base = jax.random.fold_in(key, 7)
    first, second = jax.random.split(base, 2)
    keys_drawn = jnp.clip(jax.random.normal(first, (TOKENS, D), jnp.float32), -6.0, 6.0)
    queries_drawn = jnp.clip(jax.random.normal(second, (TOKENS, D), jnp.float32), -6.0, 6.0)
    return (queries_drawn, keys_drawn)


def draw_queries(key, part):
    return query_key_pair(key)[0].astype(jnp.bfloat16)


def draw_keys(key, part):
    return query_key_pair(key)[1].astype(jnp.bfloat16)


def draw_pattern(key, part):
    tile_ids = jnp.arange(QTILES, dtype=jnp.int32)
    owner = tile_ids // QT_DEV
    lowest = jnp.maximum(owner - 1, 0) * CT_DEV
    highest = jnp.minimum(owner + 2, N_CTX) * CT_DEV
    raw_ids = jax.random.randint(jax.random.fold_in(key, 21), (QTILES, REACH), 0, 1 << 20)
    chosen_ids = lowest[:, None] + raw_ids % (highest - lowest)[:, None]
    chosen_ids = chosen_ids.at[0, 0].set(0)
    chosen_ids = chosen_ids.at[QTILES - 1, 0].set(CTILES - 1)
    return chosen_ids.astype(jnp.int32)


def draw_reached(key, part):
    counts = jax.random.randint(jax.random.fold_in(key, 33), (QTILES,), 1, REACH + 1)
    counts = counts.at[0].set(REACH)
    counts = counts.at[1].set(1)
    return counts.astype(jnp.int32)


def block_scale(rng, dims, shards, low, largest):
    loudness = 1.0
    for axis_at, parts in shards:
        steps = jax.random.uniform(jax.random.fold_in(jax.random.fold_in(rng, 6), axis_at), (parts,), jnp.float32, low / len(shards), largest / len(shards))
        loudness = loudness * jnp.repeat(jnp.exp(steps), dims[axis_at] // parts).reshape((-1,) + (1,) * (len(dims) - 1 - axis_at))
    return loudness


def centred(key, dims, spread, reach, pieces=(), kind=jnp.bfloat16):
    factor_of = block_scale(key, dims, pieces, -0.22, 0.18) if pieces else 1.0
    entries = jax.random.normal(key, dims, jnp.float32) * spread * factor_of
    return jnp.minimum(jnp.maximum(entries, -reach), reach).astype(kind)


def setup_inputs(seed: int = 0) -> dict:
    seeds = jax.random.split(jax.random.key(seed), 9)
    queries = draw_queries(jax.random.fold_in(seeds[8], 71), 0)
    keys = draw_keys(jax.random.fold_in(seeds[8], 71), 0)
    values = centred(seeds[2], (TOKENS, D), 1.0, 6.0, ((0, 512),))
    cache_keys = centred(seeds[3], (CTILES * TILE, D), 1.0, 6.0, ((0, 64), (1, 8)))
    cache_values = centred(seeds[4], (CTILES * TILE, D), 1.0, 6.0, ((0, 64), (1, 8)))
    pattern = draw_pattern(jax.random.fold_in(seeds[8], 71), 0)
    reached = draw_reached(jax.random.fold_in(seeds[8], 71), 0)
    gate = jnp.clip(jax.random.uniform(seeds[7], (D,), jnp.float32, 0.5, 2.0), 0.5, 2.0)
    return {"queries": queries, "keys": keys, "values": values, "cache_keys": cache_keys, "cache_values": cache_values, "pattern": pattern, "reached": reached, "gate": gate}


def reference(queries, keys, values, cache_keys, cache_values, pattern, reached, gate):
    score_scale = HD ** -0.5
    q_all = queries.reshape(QTILES, TILE, HEADS, HD)
    k_all = keys.reshape(QTILES, TILE, HEADS, HD)
    v_all = values.reshape(QTILES, TILE, HEADS, HD)
    cached_k = cache_keys.reshape(CTILES, TILE, HEADS, HD)
    cached_v = cache_values.reshape(CTILES, TILE, HEADS, HD)
    offsets = jnp.arange(-2, 3, dtype=jnp.int32)
    slot_ids = jnp.arange(REACH, dtype=jnp.int32)

    def one_tile(tile_index):
        near_ids = tile_index + offsets
        near_ok = (near_ids >= 0) & (near_ids < QTILES)
        near_ids = jnp.clip(near_ids, 0, QTILES - 1).astype(jnp.int32)
        row_ids = pattern[tile_index].astype(jnp.int32)
        key_blocks = jnp.concatenate([k_all[near_ids], cached_k[row_ids]], axis=0).astype(jnp.float32)
        value_blocks = jnp.concatenate([v_all[near_ids], cached_v[row_ids]], axis=0).astype(jnp.float32)
        usable_keys = jnp.concatenate([near_ok, slot_ids < reached[tile_index]])
        scores = jnp.einsum("qhd,nkhd->hqnk", q_all[tile_index].astype(jnp.float32), key_blocks,
                            precision=lax.Precision.HIGHEST) * score_scale
        keep_mask = usable_keys[None, None, :, None]
        scores = jnp.where(keep_mask, scores, -jnp.inf)
        row_peak = jnp.max(scores, axis=(2, 3), keepdims=True)
        expos = jnp.exp(scores - row_peak)
        row_total = jnp.sum(expos, axis=(2, 3))
        weights = expos.astype(jnp.bfloat16).astype(jnp.float32)
        summed = jnp.einsum("hqnk,nkhd->qhd", weights, value_blocks, precision=lax.Precision.HIGHEST)
        return (summed / jnp.transpose(row_total)[:, :, None]).reshape(TILE, HEADS * HD)

    attended = lax.map(one_tile, jnp.arange(QTILES, dtype=jnp.int32))
    return (attended.reshape(TOKENS, D) * gate).astype(jnp.bfloat16)
```

```python
import functools
import math

import jax
import jax.numpy as jnp
from jax import lax
from jax.experimental import pallas as pl
from jax.experimental.pallas import tpu as pltpu
from jax.sharding import PartitionSpec as P

HD = 128
TILE = 128
REACH = 4
NEGATIVE = -1e30
LIMIT = 24 << 20
LOG2E = math.log2(math.e)
NT = (((1,), (1,)), ((), ()))


def vmem():
    return pl.BlockSpec(memory_space=pltpu.VMEM)


def smem():
    return pl.BlockSpec(memory_space=pltpu.SMEM)


def tile_bias(pattern_ref, reached_ref, tile, cached_id, tile_count):
    row = jnp.clip(tile, 0, tile_count - 1)
    used = reached_ref[row]
    times = jnp.int32(0)
    for slot in range(REACH):
        hit = jnp.logical_and(slot < used, pattern_ref[row, slot] == cached_id)
        times = times + jnp.where(hit, 1, 0)
    bias = jnp.where(times == 1, 0.0, NEGATIVE)
    bias = jnp.where(times == 2, 1.0, bias)
    bias = jnp.where(times == 3, math.log2(3.0), bias)
    return jnp.where(times == 4, 2.0, bias)


def fill_bias(bias_ref, pattern_ref, reached_ref, rel_tiles, own_tiles, cached_tiles):
    ctx = lax.axis_index("ctx")
    tile_count = pattern_ref.shape[0]
    for row, rel in enumerate(rel_tiles):
        for t in range(own_tiles):
            near = 0.0 if abs(rel - t) <= 2 else NEGATIVE
            bias_ref[row, :, t * TILE : (t + 1) * TILE] = jnp.full((8, TILE), near, jnp.float32)
        for u in range(cached_tiles):
            bias = tile_bias(
                pattern_ref, reached_ref, ctx * own_tiles + rel, ctx * cached_tiles + u, tile_count
            )
            at = (own_tiles + u) * TILE
            bias_ref[row, :, at : at + TILE] = jnp.full((8, TILE), bias, jnp.float32)


def attend(q, k, v, ck, cv, bias):
    scale = HD**-0.5 * LOG2E
    near = lax.dot_general(q, k, NT, preferred_element_type=jnp.float32)
    far = lax.dot_general(q, ck, NT, preferred_element_type=jnp.float32)
    split = near.shape[1]
    near = near * scale + bias[:, :split]
    far = far * scale + bias[:, split:]
    peak = jnp.maximum(
        jnp.max(near, axis=1, keepdims=True), jnp.max(far, axis=1, keepdims=True)
    )
    near = jnp.exp2(near - peak)
    far = jnp.exp2(far - peak)
    total = jnp.sum(near, axis=1, keepdims=True) + jnp.sum(far, axis=1, keepdims=True)
    out = jnp.dot(near.astype(jnp.bfloat16), v, preferred_element_type=jnp.float32)
    out = out + jnp.dot(far.astype(jnp.bfloat16), cv, preferred_element_type=jnp.float32)
    return out / total, peak + jnp.log2(total)


def pieces(lse):
    high = lse.astype(jnp.bfloat16).astype(jnp.float32)
    rest = lse - high
    middle = rest.astype(jnp.bfloat16).astype(jnp.float32)
    low = rest - middle
    return (high + pltpu.roll(middle, 32, 1) + pltpu.roll(low, 64, 1)).astype(jnp.bfloat16)


def whole(block):
    block = block.astype(jnp.float32)
    return block + pltpu.roll(block, 96, 1) + pltpu.roll(block, 64, 1)


def attend_all(q_ref, kv_ref, ck_ref, cv_ref, bias_ref, first_row, put):
    parts, _, part, width = kv_ref.shape
    rows = parts * part
    lane = lax.broadcasted_iota(jnp.int32, (TILE, HD), 1)
    for t in range(rows // TILE):
        bias = bias_ref[first_row + t, 0:1, :]
        stats = jnp.zeros((TILE, HD), jnp.float32)
        for h in range(width // HD):
            cols = slice(h * HD, (h + 1) * HD)
            q = q_ref[t * TILE : (t + 1) * TILE, cols]
            k = kv_ref[:, 0, :, cols].reshape(rows, HD)
            v = kv_ref[:, 1, :, cols].reshape(rows, HD)
            out, lse = attend(q, k, v, ck_ref[:, cols], cv_ref[:, cols], bias)
            put(t, cols, out)
            stats = jnp.where(lane == h, lse, stats)
        put(t, None, stats)


def far_kernel(
    pattern_ref, reached_ref, below_ref, above_ref, kv_ref, ck_ref, cv_ref, to_below_ref, to_above_ref, bias_ref
):
    own = kv_ref.shape[0] * kv_ref.shape[2] // TILE
    rel = tuple(range(-own, 0)) + tuple(range(own, 2 * own))
    fill_bias(bias_ref, pattern_ref, reached_ref, rel, own, ck_ref.shape[0] // TILE)
    width = kv_ref.shape[3]
    for side, (q_ref, o_ref) in enumerate(((below_ref, to_below_ref), (above_ref, to_above_ref))):

        def put(t, cols, value, o_ref=o_ref):
            rows = slice(t * TILE, (t + 1) * TILE)
            if cols is None:
                o_ref[rows, width:] = pieces(value)
            else:
                o_ref[rows, cols] = value.astype(jnp.bfloat16)

        attend_all(q_ref, kv_ref, ck_ref, cv_ref, bias_ref, side * own, put)


def own_kernel(pattern_ref, reached_ref, q_ref, kv_ref, ck_ref, cv_ref, o_ref, stats_ref, bias_ref):
    own = kv_ref.shape[0] * kv_ref.shape[2] // TILE
    fill_bias(bias_ref, pattern_ref, reached_ref, tuple(range(own)), own, ck_ref.shape[0] // TILE)

    def put(t, cols, value):
        rows = slice(t * TILE, (t + 1) * TILE)
        if cols is None:
            stats_ref[rows, :] = value
        else:
            o_ref[rows, cols] = value

    attend_all(q_ref, kv_ref, ck_ref, cv_ref, bias_ref, 0, put)


def mix_kernel(count, o_ref, stats_ref, low_ref, high_ref, gate_ref, out_ref):
    ctx = lax.axis_index("ctx")
    head = lax.axis_index("head")
    rows, width = o_ref.shape
    heads = width // HD
    mine = stats_ref[...]
    low = jnp.where(ctx > 0, whole(low_ref[:, width:]), NEGATIVE)
    high = jnp.where(ctx < count - 1, whole(high_ref[:, width:]), NEGATIVE)
    peak = jnp.maximum(jnp.maximum(mine, low), high)
    mine, low, high = jnp.exp2(mine - peak), jnp.exp2(low - peak), jnp.exp2(high - peak)
    total = 1.0 / (mine + low + high)
    mine, low, high = mine * total, low * total, high * total
    for h in range(heads):
        cols = slice(h * HD, (h + 1) * HD)
        gate = gate_ref[pl.ds(head * heads + h, 1), :]
        mixed = o_ref[:, cols] * mine[:, h : h + 1]
        mixed = mixed + low_ref[:, cols].astype(jnp.float32) * low[:, h : h + 1]
        mixed = mixed + high_ref[:, cols].astype(jnp.float32) * high[:, h : h + 1]
        out_ref[:, cols] = (mixed * gate).astype(jnp.bfloat16)


def attention_cost(tiles, rows, cached, width):
    pairs = tiles * TILE * (rows + cached)
    return pl.CostEstimate(
        flops=4 * pairs * width, bytes_accessed=4 * (rows + cached) * width, transcendentals=pairs * (width // HD)
    )


def local(queries, keys, values, cache_keys, cache_values, pattern, reached, gate):
    split = lax.axis_size("head")
    count = lax.axis_size("ctx")
    part, full = queries.shape
    width = full // split
    rows = part * split
    cached = cache_keys.shape[0]
    own = rows // TILE
    up = [(i, i + 1) for i in range(count - 1)]
    down = [(i + 1, i) for i in range(count - 1)]

    def blocks(x):
        return jnp.transpose(x.reshape(part, split, width), (1, 0, 2))

    q = lax.all_to_all(blocks(queries), "head", split_axis=0, concat_axis=0, tiled=True).reshape(rows, width)
    kv = jnp.stack([blocks(keys), blocks(values)], axis=1)
    q, kv = lax.optimization_barrier((q, kv))
    from_below = lax.ppermute(q, "ctx", up)
    from_above = lax.ppermute(q, "ctx", down)
    kv = lax.all_to_all(kv, "head", split_axis=0, concat_axis=0, tiled=True)

    keys_seen = rows + cached
    partial = jax.ShapeDtypeStruct((rows, width + HD), jnp.bfloat16)
    to_below, to_above = pl.pallas_call(
        far_kernel,
        out_shape=(partial, partial),
        in_specs=[smem(), smem()] + [vmem()] * 5,
        out_specs=(vmem(), vmem()),
        scratch_shapes=[pltpu.VMEM((2 * own, 8, keys_seen), jnp.float32)],
        cost_estimate=attention_cost(2 * own, rows, cached, width),
        compiler_params=pltpu.CompilerParams(vmem_limit_bytes=LIMIT),
        name="far",
    )(pattern, reached, from_below, from_above, kv, cache_keys, cache_values)
    got_high = lax.ppermute(to_below, "ctx", down)
    got_low = lax.ppermute(to_above, "ctx", up)
    mine, stats = pl.pallas_call(
        own_kernel,
        out_shape=(
            jax.ShapeDtypeStruct((rows, width), jnp.float32),
            jax.ShapeDtypeStruct((rows, HD), jnp.float32),
        ),
        in_specs=[smem(), smem()] + [vmem()] * 4,
        out_specs=(vmem(), vmem()),
        scratch_shapes=[pltpu.VMEM((own, 8, keys_seen), jnp.float32)],
        cost_estimate=attention_cost(own, rows, cached, width),
        compiler_params=pltpu.CompilerParams(vmem_limit_bytes=LIMIT),
        name="own",
    )(pattern, reached, q, kv, cache_keys, cache_values)
    out = pl.pallas_call(
        functools.partial(mix_kernel, count),
        out_shape=jax.ShapeDtypeStruct((rows, width), jnp.bfloat16),
        in_specs=[vmem()] * 5,
        out_specs=vmem(),
        compiler_params=pltpu.CompilerParams(vmem_limit_bytes=LIMIT),
        name="mix",
    )(mine, stats, got_low, got_high, gate.reshape(full // HD, HD))
    out = lax.all_to_all(out.reshape(split, part, width), "head", split_axis=0, concat_axis=0, tiled=True)
    return jnp.transpose(out, (1, 0, 2)).reshape(part, full)


def solution(mesh):
    tokens = P(("ctx", "head"), None)
    cached = P("ctx", "head")
    return jax.shard_map(
        local,
        mesh=mesh,
        in_specs=(tokens, tokens, tokens, cached, cached, P(), P(), P()),
        out_specs=tokens,
        check_vma=False,
    )
```

```python
import functools
import math

import jax
import jax.numpy as jnp
from jax import lax
from jax.experimental import pallas as pl
from jax.experimental.pallas import tpu as pltpu
from jax.sharding import PartitionSpec as P


HD = 128
TILE = 128
REACH = 4
NEGATIVE = -1e30
LIMIT = 24 << 20
PLANE = 16
SWAPPED = 112
LOG2E = math.log2(math.e)
NT = (((1,), (1,)), ((), ()))


def vmem():
    return pl.BlockSpec(memory_space=pltpu.VMEM)


def smem():
    return pl.BlockSpec(memory_space=pltpu.SMEM)


def tile_bias(pattern_ref, reached_ref, tile, cached_id, tile_count):
    row = jnp.clip(tile, 0, tile_count - 1)
    used = reached_ref[row]
    times = jnp.int32(0)
    for slot in range(REACH):
        hit = jnp.logical_and(slot < used, pattern_ref[row, slot] == cached_id)
        times = times + jnp.where(hit, 1, 0)
    bias = jnp.where(times == 1, 0.0, NEGATIVE)
    bias = jnp.where(times == 2, 1.0, bias)
    bias = jnp.where(times == 3, math.log2(3.0), bias)
    return jnp.where(times == 4, 2.0, bias)


def fill_bias(bias_ref, pattern_ref, reached_ref, rel_tiles, own_tiles, cached_tiles):
    ctx = lax.axis_index("ctx")
    tile_count = pattern_ref.shape[0]
    for row, rel in enumerate(rel_tiles):
        for t in range(own_tiles):
            near = 0.0 if abs(rel - t) <= 2 else NEGATIVE
            bias_ref[row, :, t * TILE : (t + 1) * TILE] = jnp.full((8, TILE), near, jnp.float32)
        for u in range(cached_tiles):
            bias = tile_bias(
                pattern_ref, reached_ref, ctx * own_tiles + rel, ctx * cached_tiles + u, tile_count
            )
            at = (own_tiles + u) * TILE
            bias_ref[row, :, at : at + TILE] = jnp.full((8, TILE), bias, jnp.float32)


def attend(q, k, v, ck, cv, bias):
    scale = HD**-0.5 * LOG2E
    near = lax.dot_general(q, k, NT, preferred_element_type=jnp.float32)
    far = lax.dot_general(q, ck, NT, preferred_element_type=jnp.float32)
    split = near.shape[1]
    near = near * scale + bias[:, :split]
    far = far * scale + bias[:, split:]
    peak = jnp.maximum(
        jnp.max(near, axis=1, keepdims=True), jnp.max(far, axis=1, keepdims=True)
    )
    near = jnp.exp2(near - peak)
    far = jnp.exp2(far - peak)
    total = jnp.sum(near, axis=1, keepdims=True) + jnp.sum(far, axis=1, keepdims=True)
    out = jnp.dot(near.astype(jnp.bfloat16), v, preferred_element_type=jnp.float32)
    out = out + jnp.dot(far.astype(jnp.bfloat16), cv, preferred_element_type=jnp.float32)
    return out / total, peak + jnp.log2(total)


def pieces(lse):
    lse = jnp.transpose(lse)[:16]
    high = lse.astype(jnp.bfloat16)
    rest = lse - high.astype(jnp.float32)
    middle = rest.astype(jnp.bfloat16)
    low = (rest - middle.astype(jnp.float32)).astype(jnp.bfloat16)
    return high, middle, low


def whole(rows):
    rows = rows.astype(jnp.float32)
    lse = rows[:, :TILE] + rows[:, TILE : 2 * TILE] + rows[:, 2 * TILE :]
    return jnp.transpose(jnp.concatenate([lse] * (HD // 16), axis=0))


def attend_all(load, kv_ref, ck_ref, cv_ref, bias_ref, first_row, put):
    parts, _, part, width = kv_ref.shape
    rows = parts * part
    lane = lax.broadcasted_iota(jnp.int32, (TILE, HD), 1)
    for t in range(rows // TILE):
        bias = bias_ref[first_row + t, 0:1, :]
        stats = jnp.zeros((TILE, HD), jnp.float32)
        for h in range(width // HD):
            cols = slice(h * HD, (h + 1) * HD)
            q = load(t, cols)
            k = kv_ref[:, 0, :, cols].reshape(rows, HD)
            v = kv_ref[:, 1, :, cols].reshape(rows, HD)
            out, lse = attend(q, k, v, ck_ref[:, cols], cv_ref[:, cols], bias)
            put(t, cols, out)
            stats = jnp.where(lane == h, lse, stats)
        put(t, None, stats)


def far_kernel(
    pattern_ref,
    reached_ref,
    below_ref,
    above_ref,
    direct_ref,
    swapped_ref,
    kv_ref,
    ck_ref,
    cv_ref,
    to_below_ref,
    to_above_ref,
    to_direct_ref,
    to_swapped_ref,
    bias_ref,
):
    own = kv_ref.shape[0] * kv_ref.shape[2] // TILE
    rel = tuple(range(-own, 0)) + tuple(range(own, 2 * own))
    fill_bias(bias_ref, pattern_ref, reached_ref, rel, own, ck_ref.shape[0] // TILE)
    rows = own * TILE
    near = direct_ref.shape[0]
    at = lax.rem(lax.axis_index("ctx"), PLANE)
    sides = ((below_ref, to_below_ref, at == 0), (above_ref, to_above_ref, at == PLANE - 1))
    for side, (q_ref, o_ref, jumps) in enumerate(sides):

        def load(t, cols, q_ref=q_ref, jumps=jumps):
            low, high = t * TILE, (t + 1) * TILE
            if high <= near:
                jumped = direct_ref[low:high, cols]
            elif low >= near:
                jumped = swapped_ref[low - near : high - near, cols]
            else:
                jumped = jnp.concatenate([direct_ref[low:, cols], swapped_ref[: high - near, cols]], axis=0)
            return jnp.where(jumps, jumped, q_ref[low:high, cols])

        def put(t, cols, value, o_ref=o_ref):
            if cols is None:
                for i, piece in enumerate(pieces(value)):
                    o_ref[rows:, (3 * t + i) * TILE : (3 * t + i + 1) * TILE] = piece
            else:
                o_ref[t * TILE : (t + 1) * TILE, cols] = value.astype(jnp.bfloat16)

        attend_all(load, kv_ref, ck_ref, cv_ref, bias_ref, side * own, put)

        @pl.when(jumps)
        def _(o_ref=o_ref):
            direct = to_direct_ref.shape[0]
            to_direct_ref[...] = o_ref[:direct]
            to_swapped_ref[...] = o_ref[direct:]


def own_kernel(pattern_ref, reached_ref, q_ref, kv_ref, ck_ref, cv_ref, o_ref, stats_ref, bias_ref):
    own = kv_ref.shape[0] * kv_ref.shape[2] // TILE
    fill_bias(bias_ref, pattern_ref, reached_ref, tuple(range(own)), own, ck_ref.shape[0] // TILE)

    def put(t, cols, value):
        rows = slice(t * TILE, (t + 1) * TILE)
        if cols is None:
            stats_ref[rows, :] = value
        else:
            o_ref[rows, cols] = value

    def load(t, cols):
        return q_ref[t * TILE : (t + 1) * TILE, cols]

    attend_all(load, kv_ref, ck_ref, cv_ref, bias_ref, 0, put)


def mix_kernel(count, o_ref, stats_ref, low_ref, high_ref, direct_ref, swapped_ref, gate_ref, out_ref):
    ctx = lax.axis_index("ctx")
    at = lax.rem(ctx, PLANE)
    first, last = at == 0, at == PLANE - 1
    head = lax.axis_index("head")
    rows, width = o_ref.shape
    heads = width // HD
    near = direct_ref.shape[0]
    for t in range(rows // TILE):
        here = slice(t * TILE, (t + 1) * TILE)
        stat = slice(rows - near, None), slice(3 * t * TILE, 3 * (t + 1) * TILE)
        jumped = swapped_ref[stat]
        stat = slice(rows, None), stat[1]
        low = whole(jnp.where(first, jumped, low_ref[stat]))
        high = whole(jnp.where(last, jumped, high_ref[stat]))
        low = jnp.where(ctx > 0, low, NEGATIVE)
        high = jnp.where(ctx < count - 1, high, NEGATIVE)
        mine = stats_ref[here, :]
        peak = jnp.maximum(jnp.maximum(mine, low), high)
        mine, low, high = jnp.exp2(mine - peak), jnp.exp2(low - peak), jnp.exp2(high - peak)
        total = 1.0 / (mine + low + high)
        mine, low, high = mine * total, low * total, high * total
        for h in range(heads):
            cols = slice(h * HD, (h + 1) * HD)
            start, stop = t * TILE, (t + 1) * TILE
            if stop <= near:
                jumped = direct_ref[start:stop, cols]
            elif start >= near:
                jumped = swapped_ref[start - near : stop - near, cols]
            else:
                jumped = jnp.concatenate([direct_ref[start:, cols], swapped_ref[: stop - near, cols]], axis=0)
            gate = gate_ref[pl.ds(head * heads + h, 1), :]
            mixed = o_ref[here, cols] * mine[:, h : h + 1]
            mixed = mixed + jnp.where(first, jumped, low_ref[here, cols]).astype(jnp.float32) * low[:, h : h + 1]
            mixed = mixed + jnp.where(last, jumped, high_ref[here, cols]).astype(jnp.float32) * high[:, h : h + 1]
            out_ref[here, cols] = (mixed * gate).astype(jnp.bfloat16)


def attention_cost(tiles, rows, cached, width):
    pairs = tiles * TILE * (rows + cached)
    return pl.CostEstimate(
        flops=4 * pairs * width, bytes_accessed=4 * (rows + cached) * width, transcendentals=pairs * (width // HD)
    )


def local(queries, keys, values, cache_keys, cache_values, pattern, reached, gate):
    split = lax.axis_size("head")
    count = lax.axis_size("ctx")
    part, full = queries.shape
    width = full // split
    rows = part * split
    cached = cache_keys.shape[0]
    own = rows // TILE
    firsts = range(0, count, PLANE)
    jumps = [(first - 1, first) for first in firsts if first]
    inside = [(i, i + 1) for i in range(count - 1) if (i + 1) % PLANE]
    up = inside
    down = [(b, a) for a, b in inside]
    straight = jumps + [(b, a) for a, b in jumps]
    swap = [(a, a + 1 - PLANE) for a, _ in jumps] + [(b, b - 1 + PLANE) for _, b in jumps]
    onward = [(a + 1 - PLANE, b) for a, b in jumps] + [(b - 1 + PLANE, a) for a, b in jumps]

    def shift(x, pairs):
        return lax.ppermute(x, "ctx", pairs)

    def blocks(x):
        return jnp.transpose(x.reshape(part, split, width), (1, 0, 2))

    q = lax.all_to_all(blocks(queries), "head", split_axis=0, concat_axis=0, tiled=True).reshape(rows, width)
    kv = jnp.stack([blocks(keys), blocks(values)], axis=1)
    q, kv = lax.optimization_barrier((q, kv))
    swapped = shift(q[rows - SWAPPED :], swap)
    direct = shift(q[: rows - SWAPPED], straight)
    swapped = shift(swapped, onward)
    from_below = shift(q, up)
    from_above = shift(q, down)
    kv = lax.all_to_all(kv, "head", split_axis=0, concat_axis=0, tiled=True)

    keys_seen = rows + cached
    partial = rows + 16
    shapes = [partial, partial, partial - SWAPPED, SWAPPED]
    to_below, to_above, to_direct, to_swapped = pl.pallas_call(
        far_kernel,
        out_shape=tuple(jax.ShapeDtypeStruct((n, width), jnp.bfloat16) for n in shapes),
        in_specs=[smem(), smem()] + [vmem()] * 7,
        out_specs=(vmem(),) * 4,
        scratch_shapes=[pltpu.VMEM((2 * own, 8, keys_seen), jnp.float32)],
        cost_estimate=attention_cost(2 * own, rows, cached, width),
        compiler_params=pltpu.CompilerParams(vmem_limit_bytes=LIMIT),
        name="far",
    )(pattern, reached, from_below, from_above, direct, swapped, kv, cache_keys, cache_values)
    swapped = shift(to_swapped, swap)
    direct = shift(to_direct, straight)
    got_high = shift(to_below, down)
    got_low = shift(to_above, up)
    swapped = shift(swapped, onward)
    mine, stats = pl.pallas_call(
        own_kernel,
        out_shape=(
            jax.ShapeDtypeStruct((rows, width), jnp.float32),
            jax.ShapeDtypeStruct((rows, HD), jnp.float32),
        ),
        in_specs=[smem(), smem()] + [vmem()] * 4,
        out_specs=(vmem(), vmem()),
        scratch_shapes=[pltpu.VMEM((own, 8, keys_seen), jnp.float32)],
        cost_estimate=attention_cost(own, rows, cached, width),
        compiler_params=pltpu.CompilerParams(vmem_limit_bytes=LIMIT),
        name="own",
    )(pattern, reached, q, kv, cache_keys, cache_values)
    out = pl.pallas_call(
        functools.partial(mix_kernel, count),
        out_shape=jax.ShapeDtypeStruct((rows, width), jnp.bfloat16),
        in_specs=[vmem()] * 7,
        out_specs=vmem(),
        compiler_params=pltpu.CompilerParams(vmem_limit_bytes=LIMIT),
        name="mix",
    )(mine, stats, got_low, got_high, direct, swapped, gate.reshape(full // HD, HD))
    out = lax.all_to_all(out.reshape(split, part, width), "head", split_axis=0, concat_axis=0, tiled=True)
    return jnp.transpose(out, (1, 0, 2)).reshape(part, full)


def solution(mesh):
    tokens = P(("ctx", "head"), None)
    cached = P("ctx", "head")
    return jax.shard_map(
        local,
        mesh=mesh,
        in_specs=(tokens, tokens, tokens, cached, cached, P(), P(), P()),
        out_specs=tokens,
        check_vma=False,
    )
```

```python
import functools
import math

import jax
import jax.numpy as jnp
from jax import lax
from jax.experimental import pallas as pl
from jax.experimental.pallas import tpu as pltpu
from jax.sharding import PartitionSpec as P


HD = 128
TILE = 128
REACH = 4
NEGATIVE = -1e30
LIMIT = 24 << 20
PLANE = 16
SWAPPED = 112
LOG2E = math.log2(math.e)
NT = (((1,), (1,)), ((), ()))


def vmem():
    return pl.BlockSpec(memory_space=pltpu.VMEM)


def smem():
    return pl.BlockSpec(memory_space=pltpu.SMEM)


def tile_bias(pattern_ref, reached_ref, tile, cached_id, tile_count):
    row = jnp.clip(tile, 0, tile_count - 1)
    used = reached_ref[row]
    times = jnp.int32(0)
    for slot in range(REACH):
        hit = jnp.logical_and(slot < used, pattern_ref[row, slot] == cached_id)
        times = times + jnp.where(hit, 1, 0)
    bias = jnp.where(times == 1, 0.0, NEGATIVE)
    bias = jnp.where(times == 2, 1.0, bias)
    bias = jnp.where(times == 3, math.log2(3.0), bias)
    return jnp.where(times == 4, 2.0, bias)


def fill_bias(bias_ref, pattern_ref, reached_ref, rel_tiles, own_tiles, cached_tiles):
    ctx = lax.axis_index("ctx")
    tile_count = pattern_ref.shape[0]
    for row, rel in enumerate(rel_tiles):
        for t in range(own_tiles):
            near = jnp.where(jnp.abs(rel - t) <= 2, 0.0, NEGATIVE)
            bias_ref[row, :, t * TILE : (t + 1) * TILE] = jnp.full((8, TILE), near, jnp.float32)
        for u in range(cached_tiles):
            bias = tile_bias(
                pattern_ref, reached_ref, ctx * own_tiles + rel, ctx * cached_tiles + u, tile_count
            )
            at = (own_tiles + u) * TILE
            bias_ref[row, :, at : at + TILE] = jnp.full((8, TILE), bias, jnp.float32)


def attend(q, k, v, ck, cv, bias):
    scale = HD**-0.5 * LOG2E
    near = lax.dot_general(q, k, NT, preferred_element_type=jnp.float32)
    far = lax.dot_general(q, ck, NT, preferred_element_type=jnp.float32)
    split = near.shape[1]
    near = near * scale + bias[:, :split]
    far = far * scale + bias[:, split:]
    peak = jnp.maximum(
        jnp.max(near, axis=1, keepdims=True), jnp.max(far, axis=1, keepdims=True)
    )
    near = jnp.exp2(near - peak)
    far = jnp.exp2(far - peak)
    total = jnp.sum(near, axis=1, keepdims=True) + jnp.sum(far, axis=1, keepdims=True)
    out = jnp.dot(near.astype(jnp.bfloat16), v, preferred_element_type=jnp.float32)
    out = out + jnp.dot(far.astype(jnp.bfloat16), cv, preferred_element_type=jnp.float32)
    return out / total, peak + jnp.log2(total)


def pieces(lse):
    lse = jnp.transpose(lse)[:16]
    high = lse.astype(jnp.bfloat16)
    rest = lse - high.astype(jnp.float32)
    middle = rest.astype(jnp.bfloat16)
    low = (rest - middle.astype(jnp.float32)).astype(jnp.bfloat16)
    return high, middle, low


def whole(rows):
    rows = rows.astype(jnp.float32)
    lse = rows[:, :TILE] + rows[:, TILE : 2 * TILE] + rows[:, 2 * TILE :]
    return jnp.transpose(jnp.concatenate([lse] * (HD // 16), axis=0))


def attend_all(load, kv_ref, ck_ref, cv_ref, bias_ref, first_row, put):
    parts, _, part, width = kv_ref.shape
    rows = parts * part
    lane = lax.broadcasted_iota(jnp.int32, (TILE, HD), 1)
    for t in range(rows // TILE):
        bias = bias_ref[first_row + t, 0:1, :]
        stats = jnp.zeros((TILE, HD), jnp.float32)
        for h in range(width // HD):
            cols = slice(h * HD, (h + 1) * HD)
            q = load(t, cols)
            k = kv_ref[:, 0, :, cols].reshape(rows, HD)
            v = kv_ref[:, 1, :, cols].reshape(rows, HD)
            out, lse = attend(q, k, v, ck_ref[:, cols], cv_ref[:, cols], bias)
            put(t, cols, out)
            stats = jnp.where(lane == h, lse, stats)
        put(t, None, stats)


def put_partial(o_ref, rows, t, cols, value):
    if cols is None:
        for i, piece in enumerate(pieces(value)):
            o_ref[rows:, (3 * t + i) * TILE : (3 * t + i + 1) * TILE] = piece
    else:
        o_ref[t * TILE : (t + 1) * TILE, cols] = value.astype(jnp.bfloat16)


def far_kernel(
    pattern_ref, reached_ref, below_ref, above_ref, kv_ref, ck_ref, cv_ref, to_below_ref, to_above_ref, bias_ref
):
    own = kv_ref.shape[0] * kv_ref.shape[2] // TILE
    at = lax.rem(lax.axis_index("ctx"), PLANE)
    sides = ((below_ref, to_below_ref, at > 0, -own), (above_ref, to_above_ref, at < PLANE - 1, own))
    for q_ref, o_ref, inside, base in sides:

        @pl.when(inside)
        def _(q_ref=q_ref, o_ref=o_ref, base=base):
            rel = tuple(base + t for t in range(own))
            fill_bias(bias_ref, pattern_ref, reached_ref, rel, own, ck_ref.shape[0] // TILE)

            def load(t, cols):
                return q_ref[t * TILE : (t + 1) * TILE, cols]

            put = functools.partial(put_partial, o_ref, own * TILE)
            attend_all(load, kv_ref, ck_ref, cv_ref, bias_ref, 0, put)


def jump_kernel(
    pattern_ref,
    reached_ref,
    direct_ref,
    swapped_ref,
    kv_ref,
    ck_ref,
    cv_ref,
    to_direct_ref,
    to_swapped_ref,
    bias_ref,
    o_ref,
):
    own = kv_ref.shape[0] * kv_ref.shape[2] // TILE
    near = direct_ref.shape[0]
    at = lax.rem(lax.axis_index("ctx"), PLANE)

    @pl.when(jnp.logical_or(at == 0, at == PLANE - 1))
    def _():
        base = jnp.where(at == 0, -own, own)
        rel = tuple(base + t for t in range(own))
        fill_bias(bias_ref, pattern_ref, reached_ref, rel, own, ck_ref.shape[0] // TILE)

        def load(t, cols):
            return joined(direct_ref, swapped_ref, near, t, cols)

        put = functools.partial(put_partial, o_ref, own * TILE)
        attend_all(load, kv_ref, ck_ref, cv_ref, bias_ref, 0, put)
        direct = to_direct_ref.shape[0]
        to_direct_ref[...] = o_ref[:direct]
        to_swapped_ref[...] = o_ref[direct:]


def joined(direct_ref, swapped_ref, near, t, cols):
    low, high = t * TILE, (t + 1) * TILE
    if high <= near:
        return direct_ref[low:high, cols]
    if low >= near:
        return swapped_ref[low - near : high - near, cols]
    return jnp.concatenate([direct_ref[low:, cols], swapped_ref[: high - near, cols]], axis=0)


def own_kernel(pattern_ref, reached_ref, q_ref, kv_ref, ck_ref, cv_ref, o_ref, stats_ref, bias_ref):
    own = kv_ref.shape[0] * kv_ref.shape[2] // TILE
    fill_bias(bias_ref, pattern_ref, reached_ref, tuple(range(own)), own, ck_ref.shape[0] // TILE)

    def put(t, cols, value):
        rows = slice(t * TILE, (t + 1) * TILE)
        if cols is None:
            stats_ref[rows, :] = value
        else:
            o_ref[rows, cols] = value

    def load(t, cols):
        return q_ref[t * TILE : (t + 1) * TILE, cols]

    attend_all(load, kv_ref, ck_ref, cv_ref, bias_ref, 0, put)


def mix_kernel(count, o_ref, stats_ref, low_ref, high_ref, direct_ref, swapped_ref, gate_ref, out_ref):
    ctx = lax.axis_index("ctx")
    at = lax.rem(ctx, PLANE)
    first, last = at == 0, at == PLANE - 1
    head = lax.axis_index("head")
    rows, width = o_ref.shape
    heads = width // HD
    near = direct_ref.shape[0]
    for t in range(rows // TILE):
        here = slice(t * TILE, (t + 1) * TILE)
        stat = slice(rows - near, None), slice(3 * t * TILE, 3 * (t + 1) * TILE)
        jumped = swapped_ref[stat]
        stat = slice(rows, None), stat[1]
        low = whole(jnp.where(first, jumped, low_ref[stat]))
        high = whole(jnp.where(last, jumped, high_ref[stat]))
        low = jnp.where(ctx > 0, low, NEGATIVE)
        high = jnp.where(ctx < count - 1, high, NEGATIVE)
        mine = stats_ref[here, :]
        peak = jnp.maximum(jnp.maximum(mine, low), high)
        mine, low, high = jnp.exp2(mine - peak), jnp.exp2(low - peak), jnp.exp2(high - peak)
        total = 1.0 / (mine + low + high)
        mine, low, high = mine * total, low * total, high * total
        for h in range(heads):
            cols = slice(h * HD, (h + 1) * HD)
            jumped = joined(direct_ref, swapped_ref, near, t, cols)
            gate = gate_ref[pl.ds(head * heads + h, 1), :]
            mixed = o_ref[here, cols] * mine[:, h : h + 1]
            mixed = mixed + jnp.where(first, jumped, low_ref[here, cols]).astype(jnp.float32) * low[:, h : h + 1]
            mixed = mixed + jnp.where(last, jumped, high_ref[here, cols]).astype(jnp.float32) * high[:, h : h + 1]
            out_ref[here, cols] = (mixed * gate).astype(jnp.bfloat16)


def attention_cost(tiles, rows, cached, width):
    pairs = tiles * TILE * (rows + cached)
    return pl.CostEstimate(
        flops=4 * pairs * width, bytes_accessed=4 * (rows + cached) * width, transcendentals=pairs * (width // HD)
    )


def local(queries, keys, values, cache_keys, cache_values, pattern, reached, gate):
    split = lax.axis_size("head")
    count = lax.axis_size("ctx")
    part, full = queries.shape
    width = full // split
    rows = part * split
    cached = cache_keys.shape[0]
    own = rows // TILE
    firsts = range(0, count, PLANE)
    jumps = [(first - 1, first) for first in firsts if first]
    inside = [(i, i + 1) for i in range(count - 1) if (i + 1) % PLANE]
    up = inside
    down = [(b, a) for a, b in inside]
    straight = jumps + [(b, a) for a, b in jumps]
    swap = [(a, a + 1 - PLANE) for a, _ in jumps] + [(b, b - 1 + PLANE) for _, b in jumps]
    onward = [(a + 1 - PLANE, b) for a, b in jumps] + [(b - 1 + PLANE, a) for a, b in jumps]

    def shift(x, pairs):
        return lax.ppermute(x, "ctx", pairs)

    def blocks(x):
        return jnp.transpose(x.reshape(part, split, width), (1, 0, 2))

    q = lax.all_to_all(blocks(queries), "head", split_axis=0, concat_axis=0, tiled=True).reshape(rows, width)
    kv = jnp.stack([blocks(keys), blocks(values)], axis=1)
    q, kv = lax.optimization_barrier((q, kv))
    swapped = shift(q[rows - SWAPPED :], swap)
    direct = shift(q[: rows - SWAPPED], straight)
    swapped = shift(swapped, onward)
    from_below = shift(q, up)
    from_above = shift(q, down)
    kv = lax.all_to_all(kv, "head", split_axis=0, concat_axis=0, tiled=True)

    keys_seen = rows + cached
    partial = rows + 16

    def shapes(*counts):
        return tuple(jax.ShapeDtypeStruct((n, width), jnp.bfloat16) for n in counts)

    bias = pltpu.VMEM((own, 8, keys_seen), jnp.float32)
    to_below, to_above = pl.pallas_call(
        far_kernel,
        out_shape=shapes(partial, partial),
        in_specs=[smem(), smem()] + [vmem()] * 5,
        out_specs=(vmem(),) * 2,
        scratch_shapes=[bias],
        cost_estimate=attention_cost(2 * own, rows, cached, width),
        compiler_params=pltpu.CompilerParams(vmem_limit_bytes=LIMIT),
        name="far",
    )(pattern, reached, from_below, from_above, kv, cache_keys, cache_values)
    got_high = shift(to_below, down)
    got_low = shift(to_above, up)
    to_direct, to_swapped = pl.pallas_call(
        jump_kernel,
        out_shape=shapes(partial - SWAPPED, SWAPPED),
        in_specs=[smem(), smem()] + [vmem()] * 5,
        out_specs=(vmem(),) * 2,
        scratch_shapes=[bias, pltpu.VMEM((partial, width), jnp.bfloat16)],
        cost_estimate=attention_cost(own, rows, cached, width),
        compiler_params=pltpu.CompilerParams(vmem_limit_bytes=LIMIT),
        name="jump",
    )(pattern, reached, direct, swapped, kv, cache_keys, cache_values)
    swapped = shift(to_swapped, swap)
    direct = shift(to_direct, straight)
    swapped = shift(swapped, onward)
    mine, stats = pl.pallas_call(
        own_kernel,
        out_shape=(
            jax.ShapeDtypeStruct((rows, width), jnp.float32),
            jax.ShapeDtypeStruct((rows, HD), jnp.float32),
        ),
        in_specs=[smem(), smem()] + [vmem()] * 4,
        out_specs=(vmem(), vmem()),
        scratch_shapes=[pltpu.VMEM((own, 8, keys_seen), jnp.float32)],
        cost_estimate=attention_cost(own, rows, cached, width),
        compiler_params=pltpu.CompilerParams(vmem_limit_bytes=LIMIT),
        name="own",
    )(pattern, reached, q, kv, cache_keys, cache_values)
    out = pl.pallas_call(
        functools.partial(mix_kernel, count),
        out_shape=jax.ShapeDtypeStruct((rows, width), jnp.bfloat16),
        in_specs=[vmem()] * 7,
        out_specs=vmem(),
        compiler_params=pltpu.CompilerParams(vmem_limit_bytes=LIMIT),
        name="mix",
    )(mine, stats, got_low, got_high, direct, swapped, gate.reshape(full // HD, HD))
    out = lax.all_to_all(out.reshape(split, part, width), "head", split_axis=0, concat_axis=0, tiled=True)
    return jnp.transpose(out, (1, 0, 2)).reshape(part, full)


def solution(mesh):
    tokens = P(("ctx", "head"), None)
    cached = P("ctx", "head")
    return jax.shard_map(
        local,
        mesh=mesh,
        in_specs=(tokens, tokens, tokens, cached, cached, P(), P(), P()),
        out_specs=tokens,
        check_vma=False,
    )
```

```python
import functools
import math

import jax
import jax.numpy as jnp
from jax import lax
from jax.experimental import pallas as pl
from jax.experimental.pallas import tpu as pltpu
from jax.sharding import PartitionSpec as P


HD = 128
TILE = 128
REACH = 4
NEGATIVE = -1e30
LIMIT = 24 << 20
PLANE = 16
SIDE = 4
DETOUR = 80
LOG2E = math.log2(math.e)
NT = (((1,), (1,)), ((), ()))


def vmem():
    return pl.BlockSpec(memory_space=pltpu.VMEM)


def smem():
    return pl.BlockSpec(memory_space=pltpu.SMEM)


def times_named(pattern_ref, reached_ref, tile, cached_id):
    row = jnp.clip(tile, 0, pattern_ref.shape[0] - 1)
    used = reached_ref[row]
    times = jnp.int32(0)
    for slot in range(REACH):
        hit = jnp.logical_and(slot < used, pattern_ref[row, slot] == cached_id)
        times = times + jnp.where(hit, 1, 0)
    return times


def scores_of(q, k):
    return lax.dot_general(q, k, NT, preferred_element_type=jnp.float32) * (HD**-0.5 * LOG2E)


def pieces(lse):
    lse = jnp.transpose(lse)[:16]
    high = lse.astype(jnp.bfloat16)
    rest = lse - high.astype(jnp.float32)
    middle = rest.astype(jnp.bfloat16)
    low = (rest - middle.astype(jnp.float32)).astype(jnp.bfloat16)
    return high, middle, low


def whole(rows):
    rows = rows.astype(jnp.float32)
    lse = rows[:, :TILE] + rows[:, TILE : 2 * TILE] + rows[:, 2 * TILE :]
    return jnp.transpose(jnp.concatenate([lse] * (HD // 16), axis=0))


def attend_all(load, rel_tiles, refs, put):
    pattern_ref, reached_ref, kv_ref, ck_ref, cv_ref, peak_ref, total_ref, sum_ref = refs
    parts, _, part, width = kv_ref.shape
    rows = parts * part
    own, cached, heads = rows // TILE, ck_ref.shape[0] // TILE, width // HD
    ctx = lax.axis_index("ctx")
    lane = lax.broadcasted_iota(jnp.int32, (TILE, HD), 1)
    for t, rel in enumerate(rel_tiles):
        near = [abs(rel - i) <= 2 if isinstance(rel, int) else None for i in range(own)]
        kept = [i for i, ok in enumerate(near) if ok is not False]
        seen = slice(kept[0], kept[-1] + 1)
        low, high = seen.start * TILE, seen.stop * TILE
        bias = None
        if None in near:
            ok = [jnp.where(jnp.abs(rel - i) <= 2, 0.0, NEGATIVE) for i in range(own)]
            bias = jnp.concatenate([jnp.full((1, TILE), one, jnp.float32) for one in ok], axis=1)
        for h in range(heads):
            cols = slice(h * HD, (h + 1) * HD)
            k = kv_ref[:, 0, :, cols].reshape(rows, HD)[low:high]
            v = kv_ref[:, 1, :, cols].reshape(rows, HD)[low:high]
            scores = scores_of(load(t, cols), k)
            if bias is not None:
                scores = scores + bias
            peak = jnp.max(scores, axis=1, keepdims=True)
            expos = jnp.exp2(scores - peak)
            total = jnp.sum(expos, axis=1, keepdims=True)
            sum_ref[h] = jnp.dot(expos.astype(jnp.bfloat16), v, preferred_element_type=jnp.float32)
            peak_ref[h] = jnp.broadcast_to(peak, (TILE, HD))
            total_ref[h] = jnp.broadcast_to(total, (TILE, HD))
        for u in range(cached):
            times = times_named(pattern_ref, reached_ref, ctx * own + rel, ctx * cached + u)

            @pl.when(times > 0)
            def _(t=t, u=u, times=times):
                log = jnp.where(times == 2, 1.0, jnp.where(times == 3, math.log2(3.0), 0.0))
                log = jnp.where(times == 4, 2.0, log)
                there = slice(u * TILE, (u + 1) * TILE)
                for h in range(heads):
                    cols = slice(h * HD, (h + 1) * HD)
                    scores = scores_of(load(t, cols), ck_ref[there, cols]) + log
                    old = peak_ref[h]
                    peak = jnp.maximum(old, jnp.max(scores, axis=1, keepdims=True))
                    factor = jnp.exp2(old - peak)
                    expos = jnp.exp2(scores - peak)
                    peak_ref[h] = peak
                    total_ref[h] = total_ref[h] * factor + jnp.sum(expos, axis=1, keepdims=True)
                    more = jnp.dot(expos.astype(jnp.bfloat16), cv_ref[there, cols], preferred_element_type=jnp.float32)
                    sum_ref[h] = sum_ref[h] * factor + more

        stats = jnp.zeros((TILE, HD), jnp.float32)
        for h in range(heads):
            total = total_ref[h]
            put(t, slice(h * HD, (h + 1) * HD), sum_ref[h] / total)
            stats = jnp.where(lane == h, peak_ref[h] + jnp.log2(total), stats)
        put(t, None, stats)


def put_partial(o_ref, rows, t, cols, value):
    if cols is None:
        for i, piece in enumerate(pieces(value)):
            o_ref[rows:, (3 * t + i) * TILE : (3 * t + i + 1) * TILE] = piece
    else:
        o_ref[t * TILE : (t + 1) * TILE, cols] = value.astype(jnp.bfloat16)


def far_kernel(
    pattern_ref, reached_ref, below_ref, above_ref, kv_ref, ck_ref, cv_ref, to_below_ref, to_above_ref, *scratch
):
    own = kv_ref.shape[0] * kv_ref.shape[2] // TILE
    refs = (pattern_ref, reached_ref, kv_ref, ck_ref, cv_ref, *scratch)
    at = lax.rem(lax.axis_index("ctx"), PLANE)
    sides = ((below_ref, to_below_ref, at > 0, -own), (above_ref, to_above_ref, at < PLANE - 1, own))
    for q_ref, o_ref, inside, base in sides:

        @pl.when(inside)
        def _(q_ref=q_ref, o_ref=o_ref, base=base):
            def load(t, cols):
                return q_ref[t * TILE : (t + 1) * TILE, cols]

            put = functools.partial(put_partial, o_ref, own * TILE)
            attend_all(load, [base + t for t in range(own)], refs, put)


def jump_kernel(*args):
    pattern_ref, reached_ref, *given = args[:5]
    kv_ref, _, _ = args[5:8]
    taken, o_ref, refs = args[8:11], args[11], (pattern_ref, reached_ref, *args[5:8], *args[12:])
    own = kv_ref.shape[0] * kv_ref.shape[2] // TILE
    at = lax.rem(lax.axis_index("ctx"), PLANE)

    @pl.when(jnp.logical_or(at == 0, at == PLANE - 1))
    def _():
        base = jnp.where(at == 0, -own, own)

        def load(t, cols):
            return joined(given, slice(t * TILE, (t + 1) * TILE), cols)

        put = functools.partial(put_partial, o_ref, own * TILE)
        attend_all(load, [base + t for t in range(own)], refs, put)
        first = 0
        for ref in taken:
            ref[...] = o_ref[first : first + ref.shape[0]]
            first += ref.shape[0]


def joined(refs, rows, cols):
    found, first = [], 0
    for ref in refs:
        low, high = max(rows.start - first, 0), min(rows.stop - first, ref.shape[0])
        if low < high:
            found.append(ref[low:high, cols])
        first += ref.shape[0]
    return found[0] if len(found) == 1 else jnp.concatenate(found, axis=0)


def own_kernel(pattern_ref, reached_ref, q_ref, kv_ref, ck_ref, cv_ref, o_ref, stats_ref, *scratch):
    own = kv_ref.shape[0] * kv_ref.shape[2] // TILE

    def put(t, cols, value):
        rows = slice(t * TILE, (t + 1) * TILE)
        if cols is None:
            stats_ref[rows, :] = value
        else:
            o_ref[rows, cols] = value

    def load(t, cols):
        return q_ref[t * TILE : (t + 1) * TILE, cols]

    attend_all(load, list(range(own)), (pattern_ref, reached_ref, kv_ref, ck_ref, cv_ref, *scratch), put)


def mix_kernel(count, o_ref, stats_ref, low_ref, high_ref, part0_ref, part1_ref, part2_ref, gate_ref, out_ref):
    parts = (part0_ref, part1_ref, part2_ref)
    ctx = lax.axis_index("ctx")
    at = lax.rem(ctx, PLANE)
    first, last = at == 0, at == PLANE - 1
    head = lax.axis_index("head")
    rows, width = o_ref.shape
    heads = width // HD
    for t in range(rows // TILE):
        here = slice(t * TILE, (t + 1) * TILE)
        stat = slice(rows, rows + 16), slice(3 * t * TILE, 3 * (t + 1) * TILE)
        jumped = joined(parts, *stat)
        low = whole(jnp.where(first, jumped, low_ref[stat]))
        high = whole(jnp.where(last, jumped, high_ref[stat]))
        low = jnp.where(ctx > 0, low, NEGATIVE)
        high = jnp.where(ctx < count - 1, high, NEGATIVE)
        mine = stats_ref[here, :]
        peak = jnp.maximum(jnp.maximum(mine, low), high)
        mine, low, high = jnp.exp2(mine - peak), jnp.exp2(low - peak), jnp.exp2(high - peak)
        total = 1.0 / (mine + low + high)
        mine, low, high = mine * total, low * total, high * total
        for h in range(heads):
            cols = slice(h * HD, (h + 1) * HD)
            jumped = joined(parts, here, cols)
            gate = gate_ref[pl.ds(head * heads + h, 1), :]
            mixed = o_ref[here, cols] * mine[:, h : h + 1]
            mixed = mixed + jnp.where(first, jumped, low_ref[here, cols]).astype(jnp.float32) * low[:, h : h + 1]
            mixed = mixed + jnp.where(last, jumped, high_ref[here, cols]).astype(jnp.float32) * high[:, h : h + 1]
            out_ref[here, cols] = (mixed * gate).astype(jnp.bfloat16)


def attention_cost(tiles, rows, cached, width):
    pairs = tiles * TILE * (rows + cached)
    return pl.CostEstimate(
        flops=4 * pairs * width, bytes_accessed=4 * (rows + cached) * width, transcendentals=pairs * (width // HD)
    )


def local(queries, keys, values, cache_keys, cache_values, pattern, reached, gate):
    split = lax.axis_size("head")
    count = lax.axis_size("ctx")
    part, full = queries.shape
    width = full // split
    rows = part * split
    cached = cache_keys.shape[0]
    own = rows // TILE
    jumps = [(first - 1, first) for first in range(PLANE, count, PLANE)]
    corners = (PLANE - SIDE, SIDE - 1)
    up = [(i, i + 1) for i in range(count - 1) if (i + 1) % PLANE]
    down = [(b, a) for a, b in up]
    straight = jumps + [(b, a) for a, b in jumps]
    out, onward = [], []
    for rising, falling in (corners, corners[::-1]):
        ways = [(a, a + 1 - PLANE + rising, b) for a, b in jumps] + [(b, b + falling, a) for a, b in jumps]
        out.append([way[:2] for way in ways])
        onward.append([way[1:] for way in ways])

    def jump(x):
        return [shift(x[0], straight)] + [shift(shift(x[1 + i], out[i]), onward[i]) for i in range(2)]

    def shift(x, pairs):
        return lax.ppermute(x, "ctx", pairs)

    def blocks(x):
        return jnp.transpose(x.reshape(part, split, width), (1, 0, 2))

    q = lax.all_to_all(blocks(queries), "head", split_axis=0, concat_axis=0, tiled=True).reshape(rows, width)
    kv = jnp.stack([blocks(keys), blocks(values)], axis=1)
    q, kv = lax.optimization_barrier((q, kv))
    cuts = (rows - 2 * DETOUR, rows - DETOUR)
    jumped = jump([q[: cuts[0]], q[cuts[0] : cuts[1]], q[cuts[1] :]])
    from_below = shift(q, up)
    from_above = shift(q, down)
    kv = lax.all_to_all(kv, "head", split_axis=0, concat_axis=0, tiled=True)

    partial = rows + 16

    def shapes(*counts):
        return tuple(jax.ShapeDtypeStruct((n, width), jnp.bfloat16) for n in counts)

    running = [pltpu.VMEM((width // HD, TILE, HD), jnp.float32)] * 3
    to_below, to_above = pl.pallas_call(
        far_kernel,
        out_shape=shapes(partial, partial),
        in_specs=[smem(), smem()] + [vmem()] * 5,
        out_specs=(vmem(),) * 2,
        scratch_shapes=running,
        cost_estimate=attention_cost(2 * own, rows, cached, width),
        compiler_params=pltpu.CompilerParams(vmem_limit_bytes=LIMIT),
        name="far",
    )(pattern, reached, from_below, from_above, kv, cache_keys, cache_values)
    got_high = shift(to_below, down)
    got_low = shift(to_above, up)
    jumped = pl.pallas_call(
        jump_kernel,
        out_shape=shapes(partial - 2 * DETOUR, DETOUR, DETOUR),
        in_specs=[smem(), smem()] + [vmem()] * 6,
        out_specs=(vmem(),) * 3,
        scratch_shapes=[pltpu.VMEM((partial, width), jnp.bfloat16), *running],
        cost_estimate=attention_cost(own, rows, cached, width),
        compiler_params=pltpu.CompilerParams(vmem_limit_bytes=LIMIT),
        name="jump",
    )(pattern, reached, *jumped, kv, cache_keys, cache_values)
    jumped = jump(jumped)
    mine, stats = pl.pallas_call(
        own_kernel,
        out_shape=(
            jax.ShapeDtypeStruct((rows, width), jnp.float32),
            jax.ShapeDtypeStruct((rows, HD), jnp.float32),
        ),
        in_specs=[smem(), smem()] + [vmem()] * 4,
        out_specs=(vmem(), vmem()),
        scratch_shapes=running,
        cost_estimate=attention_cost(own, rows, cached, width),
        compiler_params=pltpu.CompilerParams(vmem_limit_bytes=LIMIT),
        name="own",
    )(pattern, reached, q, kv, cache_keys, cache_values)
    out = pl.pallas_call(
        functools.partial(mix_kernel, count),
        out_shape=jax.ShapeDtypeStruct((rows, width), jnp.bfloat16),
        in_specs=[vmem()] * 8,
        out_specs=vmem(),
        compiler_params=pltpu.CompilerParams(vmem_limit_bytes=LIMIT),
        name="mix",
    )(mine, stats, got_low, got_high, *jumped, gate.reshape(full // HD, HD))
    out = lax.all_to_all(out.reshape(split, part, width), "head", split_axis=0, concat_axis=0, tiled=True)
    return jnp.transpose(out, (1, 0, 2)).reshape(part, full)


def solution(mesh):
    tokens = P(("ctx", "head"), None)
    cached = P("ctx", "head")
    return jax.shard_map(
        local,
        mesh=mesh,
        in_specs=(tokens, tokens, tokens, cached, cached, P(), P(), P()),
        out_specs=tokens,
        check_vma=False,
    )
```

```python
import functools
import math

import jax
import jax.numpy as jnp
from jax import lax
from jax.experimental import pallas as pl
from jax.experimental.pallas import tpu as pltpu
from jax.sharding import PartitionSpec as P


HD = 128
TILE = 128
REACH = 4
NEGATIVE = -1e30
LIMIT = 16 << 20
PLANE = 16
SIDE = 4
Q_DETOUR = 96
O_DETOUR = 80
LOG2E = math.log2(math.e)
NT = (((1,), (1,)), ((), ()))


def vmem():
    return pl.BlockSpec(memory_space=pltpu.VMEM)


def smem():
    return pl.BlockSpec(memory_space=pltpu.SMEM)


def tile_bias(pattern_ref, reached_ref, tile, cached_id, tile_count):
    row = jnp.clip(tile, 0, tile_count - 1)
    used = reached_ref[row]
    times = jnp.int32(0)
    for slot in range(REACH):
        hit = jnp.logical_and(slot < used, pattern_ref[row, slot] == cached_id)
        times = times + jnp.where(hit, 1, 0)
    bias = jnp.where(times == 1, 0.0, NEGATIVE)
    bias = jnp.where(times == 2, 1.0, bias)
    bias = jnp.where(times == 3, math.log2(3.0), bias)
    return jnp.where(times == 4, 2.0, bias)


def fill_bias(bias_ref, pattern_ref, reached_ref, rel_tiles, own_tiles, cached_tiles):
    ctx = lax.axis_index("ctx")
    tile_count = pattern_ref.shape[0]
    for row, rel in enumerate(rel_tiles):
        for t in range(own_tiles):
            near = jnp.where(jnp.abs(rel - t) <= 2, 0.0, NEGATIVE)
            bias_ref[row, :, t * TILE : (t + 1) * TILE] = jnp.full((8, TILE), near, jnp.float32)
        for u in range(cached_tiles):
            bias = tile_bias(
                pattern_ref, reached_ref, ctx * own_tiles + rel, ctx * cached_tiles + u, tile_count
            )
            at = (own_tiles + u) * TILE
            bias_ref[row, :, at : at + TILE] = jnp.full((8, TILE), bias, jnp.float32)


def biased(scores, bias):
    scale = HD**-0.5 * LOG2E
    tiles = [scores[t * TILE : (t + 1) * TILE] * scale + row for t, row in enumerate(bias)]
    return jnp.concatenate(tiles, axis=0)


def attend(q, k, v, ck, cv, bias):
    near = lax.dot_general(q, k, NT, preferred_element_type=jnp.float32)
    far = lax.dot_general(q, ck, NT, preferred_element_type=jnp.float32)
    split = near.shape[1]
    near = biased(near, [row[:, :split] for row in bias])
    far = biased(far, [row[:, split:] for row in bias])
    peak = jnp.maximum(
        jnp.max(near, axis=1, keepdims=True), jnp.max(far, axis=1, keepdims=True)
    )
    near = jnp.exp2(near - peak)
    far = jnp.exp2(far - peak)
    total = jnp.sum(near, axis=1, keepdims=True) + jnp.sum(far, axis=1, keepdims=True)
    out = jnp.dot(near.astype(jnp.bfloat16), v, preferred_element_type=jnp.float32)
    out = out + jnp.dot(far.astype(jnp.bfloat16), cv, preferred_element_type=jnp.float32)
    return out / total, peak + jnp.log2(total)


def pieces(lse):
    lse = jnp.transpose(lse)[:16]
    high = lse.astype(jnp.bfloat16)
    rest = lse - high.astype(jnp.float32)
    middle = rest.astype(jnp.bfloat16)
    low = (rest - middle.astype(jnp.float32)).astype(jnp.bfloat16)
    return high, middle, low


def whole(rows):
    rows = rows.astype(jnp.float32)
    lse = rows[:, :TILE] + rows[:, TILE : 2 * TILE] + rows[:, 2 * TILE :]
    return jnp.transpose(jnp.concatenate([lse] * (HD // 16), axis=0))


def attend_all(load, rel_tiles, refs, put):
    pattern_ref, reached_ref, kv_ref, ck_ref, cv_ref, bias_ref = refs
    parts, _, part, width = kv_ref.shape
    rows = parts * part
    fill_bias(bias_ref, pattern_ref, reached_ref, rel_tiles, rows // TILE, ck_ref.shape[0] // TILE)
    bias = [bias_ref[t, 0:1, :] for t in range(rows // TILE)]
    lane = lax.broadcasted_iota(jnp.int32, (rows, HD), 1)
    stats = jnp.zeros((rows, HD), jnp.float32)
    for h in range(width // HD):
        cols = slice(h * HD, (h + 1) * HD)
        k = kv_ref[:, 0, :, cols].reshape(rows, HD)
        v = kv_ref[:, 1, :, cols].reshape(rows, HD)
        out, lse = attend(load(cols), k, v, ck_ref[:, cols], cv_ref[:, cols], bias)
        put(cols, out)
        stats = jnp.where(lane == h, lse, stats)
    put(None, stats)


def put_partial(o_ref, rows, cols, value):
    if cols is not None:
        o_ref[:rows, cols] = value.astype(jnp.bfloat16)
        return
    for t in range(rows // TILE):
        for i, piece in enumerate(pieces(value[t * TILE : (t + 1) * TILE])):
            o_ref[rows:, (3 * t + i) * TILE : (3 * t + i + 1) * TILE] = piece


def far_kernel(
    pattern_ref, reached_ref, below_ref, above_ref, kv_ref, ck_ref, cv_ref, to_below_ref, to_above_ref, *scratch
):
    own = kv_ref.shape[0] * kv_ref.shape[2] // TILE
    refs = (pattern_ref, reached_ref, kv_ref, ck_ref, cv_ref, *scratch)
    at = lax.rem(lax.axis_index("ctx"), PLANE)
    sides = ((below_ref, to_below_ref, at > 0, -own), (above_ref, to_above_ref, at < PLANE - 1, own))
    for q_ref, o_ref, inside, base in sides:

        @pl.when(inside)
        def _(q_ref=q_ref, o_ref=o_ref, base=base):
            def load(cols):
                return q_ref[:, cols]

            put = functools.partial(put_partial, o_ref, own * TILE)
            attend_all(load, [base + t for t in range(own)], refs, put)


def jump_kernel(*args):
    pattern_ref, reached_ref, *given = args[:5]
    kv_ref, _, _ = args[5:8]
    taken, o_ref, refs = args[8:11], args[11], (pattern_ref, reached_ref, *args[5:8], *args[12:])
    own = kv_ref.shape[0] * kv_ref.shape[2] // TILE
    at = lax.rem(lax.axis_index("ctx"), PLANE)

    @pl.when(jnp.logical_or(at == 0, at == PLANE - 1))
    def _():
        base = jnp.where(at == 0, -own, own)

        def load(cols):
            return joined(given, slice(0, own * TILE), cols)

        put = functools.partial(put_partial, o_ref, own * TILE)
        attend_all(load, [base + t for t in range(own)], refs, put)
        first = 0
        for ref in taken:
            ref[...] = o_ref[first : first + ref.shape[0]]
            first += ref.shape[0]


def joined(refs, rows, cols):
    found, first = [], 0
    for ref in refs:
        low, high = max(rows.start - first, 0), min(rows.stop - first, ref.shape[0])
        if low < high:
            found.append(ref[low:high, cols])
        first += ref.shape[0]
    return found[0] if len(found) == 1 else jnp.concatenate(found, axis=0)


def own_kernel(pattern_ref, reached_ref, q_ref, kv_ref, ck_ref, cv_ref, o_ref, stats_ref, bias_ref):
    def put(cols, value):
        if cols is None:
            stats_ref[...] = value
        else:
            o_ref[:, cols] = value

    own = kv_ref.shape[0] * kv_ref.shape[2] // TILE
    refs = (pattern_ref, reached_ref, kv_ref, ck_ref, cv_ref, bias_ref)
    attend_all(lambda cols: q_ref[:, cols], list(range(own)), refs, put)


def mix_kernel(count, o_ref, stats_ref, low_ref, high_ref, part0_ref, part1_ref, part2_ref, gate_ref, out_ref):
    parts = (part0_ref, part1_ref, part2_ref)
    ctx = lax.axis_index("ctx")
    at = lax.rem(ctx, PLANE)
    first, last = at == 0, at == PLANE - 1
    head = lax.axis_index("head")
    rows, width = o_ref.shape
    heads = width // HD
    for t in range(rows // TILE):
        here = slice(t * TILE, (t + 1) * TILE)
        stat = slice(rows, rows + 16), slice(3 * t * TILE, 3 * (t + 1) * TILE)
        jumped = joined(parts, *stat)
        low = whole(jnp.where(first, jumped, low_ref[stat]))
        high = whole(jnp.where(last, jumped, high_ref[stat]))
        low = jnp.where(ctx > 0, low, NEGATIVE)
        high = jnp.where(ctx < count - 1, high, NEGATIVE)
        mine = stats_ref[here, :]
        peak = jnp.maximum(jnp.maximum(mine, low), high)
        mine, low, high = jnp.exp2(mine - peak), jnp.exp2(low - peak), jnp.exp2(high - peak)
        total = 1.0 / (mine + low + high)
        mine, low, high = mine * total, low * total, high * total
        for h in range(heads):
            cols = slice(h * HD, (h + 1) * HD)
            jumped = joined(parts, here, cols)
            gate = gate_ref[pl.ds(head * heads + h, 1), :]
            mixed = o_ref[here, cols] * mine[:, h : h + 1]
            mixed = mixed + jnp.where(first, jumped, low_ref[here, cols]).astype(jnp.float32) * low[:, h : h + 1]
            mixed = mixed + jnp.where(last, jumped, high_ref[here, cols]).astype(jnp.float32) * high[:, h : h + 1]
            out_ref[here, cols] = (mixed * gate).astype(jnp.bfloat16)


def split_kernel(x_ref, out_ref, sems):
    count, _, width = out_ref.shape
    copies = [
        pltpu.make_async_copy(x_ref.at[:, i * width : (i + 1) * width], out_ref.at[i], sems.at[i]) for i in range(count)
    ]
    for copy in copies:
        copy.start()
    for copy in copies:
        copy.wait()


def attention_cost(tiles, rows, cached, width):
    pairs = tiles * TILE * (rows + cached)
    return pl.CostEstimate(
        flops=4 * pairs * width, bytes_accessed=4 * (rows + cached) * width, transcendentals=pairs * (width // HD)
    )


def local(queries, keys, values, cache_keys, cache_values, pattern, reached, gate):
    split = lax.axis_size("head")
    count = lax.axis_size("ctx")
    part, full = queries.shape
    width = full // split
    rows = part * split
    cached = cache_keys.shape[0]
    own = rows // TILE
    jumps = [(first - 1, first) for first in range(PLANE, count, PLANE)]
    corners = (PLANE - SIDE, SIDE - 1)
    up = [(i, i + 1) for i in range(count - 1) if (i + 1) % PLANE]
    down = [(b, a) for a, b in up]
    straight = jumps + [(b, a) for a, b in jumps]
    out, onward = [], []
    for rising, falling in (corners, corners[::-1]):
        ways = [(a, a + 1 - PLANE + rising, b) for a, b in jumps] + [(b, b + falling, a) for a, b in jumps]
        out.append([way[:2] for way in ways])
        onward.append([way[1:] for way in ways])

    def jump(x):
        return [shift(x[0], straight)] + [shift(shift(x[1 + i], out[i]), onward[i]) for i in range(2)]

    def shift(x, pairs):
        return lax.ppermute(x, "ctx", pairs)

    def blocks(x):
        return jnp.transpose(x.reshape(part, split, width), (1, 0, 2))

    q = pl.pallas_call(
        split_kernel,
        out_shape=jax.ShapeDtypeStruct((split, part, width), jnp.bfloat16),
        in_specs=[pl.BlockSpec(memory_space=pltpu.HBM)],
        out_specs=vmem(),
        scratch_shapes=[pltpu.SemaphoreType.DMA((split,))],
        compiler_params=pltpu.CompilerParams(vmem_limit_bytes=60 << 20),
        name="split",
    )(queries)
    q = lax.all_to_all(q, "head", split_axis=0, concat_axis=0, tiled=True).reshape(rows, width)
    kv = jnp.stack([blocks(keys), blocks(values)], axis=1)
    q, kv = lax.optimization_barrier((q, kv))
    cuts = (rows - 2 * Q_DETOUR, rows - Q_DETOUR)
    jumped = jump([q[: cuts[0]], q[cuts[0] : cuts[1]], q[cuts[1] :]])
    from_below = shift(q, up)
    from_above = shift(q, down)
    kv = lax.all_to_all(kv, "head", split_axis=0, concat_axis=0, tiled=True)

    partial = rows + 16

    def shapes(*counts):
        return tuple(jax.ShapeDtypeStruct((n, width), jnp.bfloat16) for n in counts)

    bias = pltpu.VMEM((own, 8, rows + cached), jnp.float32)
    to_below, to_above = pl.pallas_call(
        far_kernel,
        out_shape=shapes(partial, partial),
        in_specs=[smem(), smem()] + [vmem()] * 5,
        out_specs=(vmem(),) * 2,
        scratch_shapes=[bias],
        cost_estimate=attention_cost(2 * own, rows, cached, width),
        compiler_params=pltpu.CompilerParams(vmem_limit_bytes=LIMIT),
        name="far",
    )(pattern, reached, from_below, from_above, kv, cache_keys, cache_values)
    got_high = shift(to_below, down)
    got_low = shift(to_above, up)
    jumped = pl.pallas_call(
        jump_kernel,
        out_shape=shapes(partial - 2 * O_DETOUR, O_DETOUR, O_DETOUR),
        in_specs=[smem(), smem()] + [vmem()] * 6,
        out_specs=(vmem(),) * 3,
        scratch_shapes=[pltpu.VMEM((partial, width), jnp.bfloat16), bias],
        cost_estimate=attention_cost(own, rows, cached, width),
        compiler_params=pltpu.CompilerParams(vmem_limit_bytes=LIMIT),
        name="jump",
    )(pattern, reached, *jumped, kv, cache_keys, cache_values)
    jumped = jump(jumped)
    mine, stats = pl.pallas_call(
        own_kernel,
        out_shape=(
            jax.ShapeDtypeStruct((rows, width), jnp.float32),
            jax.ShapeDtypeStruct((rows, HD), jnp.float32),
        ),
        in_specs=[smem(), smem()] + [vmem()] * 4,
        out_specs=(vmem(), vmem()),
        scratch_shapes=[bias],
        cost_estimate=attention_cost(own, rows, cached, width),
        compiler_params=pltpu.CompilerParams(vmem_limit_bytes=LIMIT),
        name="own",
    )(pattern, reached, q, kv, cache_keys, cache_values)
    out = pl.pallas_call(
        functools.partial(mix_kernel, count),
        out_shape=jax.ShapeDtypeStruct((rows, width), jnp.bfloat16),
        in_specs=[vmem()] * 8,
        out_specs=vmem(),
        compiler_params=pltpu.CompilerParams(vmem_limit_bytes=LIMIT),
        name="mix",
    )(mine, stats, got_low, got_high, *jumped, gate.reshape(full // HD, HD))
    out = lax.all_to_all(out.reshape(split, part, width), "head", split_axis=0, concat_axis=0, tiled=True)
    return jnp.transpose(out, (1, 0, 2)).reshape(part, full)


def solution(mesh):
    tokens = P(("ctx", "head"), None)
    cached = P("ctx", "head")
    return jax.shard_map(
        local,
        mesh=mesh,
        in_specs=(tokens, tokens, tokens, cached, cached, P(), P(), P()),
        out_specs=tokens,
        check_vma=False,
    )
```

```python
import functools
import math

import jax
import jax.numpy as jnp
from jax import lax
from jax.experimental import pallas as pl
from jax.experimental.pallas import tpu as pltpu
from jax.sharding import PartitionSpec as P


HD = 128
TILE = 128
REACH = 4
NEGATIVE = -1e30
LIMIT = 16 << 20
PLANE = 16
SIDE = 4
DETOUR = 96
LOG2E = math.log2(math.e)
NT = (((1,), (1,)), ((), ()))


def vmem():
    return pl.BlockSpec(memory_space=pltpu.VMEM)


def smem():
    return pl.BlockSpec(memory_space=pltpu.SMEM)


def tile_bias(pattern_ref, reached_ref, tile, cached_id, tile_count):
    row = jnp.clip(tile, 0, tile_count - 1)
    used = reached_ref[row]
    times = jnp.int32(0)
    for slot in range(REACH):
        hit = jnp.logical_and(slot < used, pattern_ref[row, slot] == cached_id)
        times = times + jnp.where(hit, 1, 0)
    bias = jnp.where(times == 1, 0.0, NEGATIVE)
    bias = jnp.where(times == 2, 1.0, bias)
    bias = jnp.where(times == 3, math.log2(3.0), bias)
    return jnp.where(times == 4, 2.0, bias)


def fill_bias(bias_ref, pattern_ref, reached_ref, rel_tiles, own_tiles, cached_tiles):
    ctx = lax.axis_index("ctx")
    tile_count = pattern_ref.shape[0]
    for row, rel in enumerate(rel_tiles):
        for t in range(own_tiles):
            near = jnp.where(jnp.abs(rel - t) <= 2, 0.0, NEGATIVE)
            bias_ref[row, :, t * TILE : (t + 1) * TILE] = jnp.full((8, TILE), near, jnp.float32)
        for u in range(cached_tiles):
            bias = tile_bias(
                pattern_ref, reached_ref, ctx * own_tiles + rel, ctx * cached_tiles + u, tile_count
            )
            at = (own_tiles + u) * TILE
            bias_ref[row, :, at : at + TILE] = jnp.full((8, TILE), bias, jnp.float32)


def biased(scores, bias):
    scale = HD**-0.5 * LOG2E
    tiles = [scores[t * TILE : (t + 1) * TILE] * scale + row for t, row in enumerate(bias)]
    return jnp.concatenate(tiles, axis=0)


def attend(q, k, v, ck, cv, bias):
    near = lax.dot_general(q, k, NT, preferred_element_type=jnp.float32)
    far = lax.dot_general(q, ck, NT, preferred_element_type=jnp.float32)
    split = near.shape[1]
    near = biased(near, [row[:, :split] for row in bias])
    far = biased(far, [row[:, split:] for row in bias])
    peak = jnp.maximum(
        jnp.max(near, axis=1, keepdims=True), jnp.max(far, axis=1, keepdims=True)
    )
    near = jnp.exp2(near - peak)
    far = jnp.exp2(far - peak)
    total = jnp.sum(near, axis=1, keepdims=True) + jnp.sum(far, axis=1, keepdims=True)
    out = jnp.dot(near.astype(jnp.bfloat16), v, preferred_element_type=jnp.float32)
    out = out + jnp.dot(far.astype(jnp.bfloat16), cv, preferred_element_type=jnp.float32)
    return out / total, peak + jnp.log2(total)


def pieces(lse):
    lse = jnp.transpose(lse)[:16]
    high = lse.astype(jnp.bfloat16)
    rest = lse - high.astype(jnp.float32)
    middle = rest.astype(jnp.bfloat16)
    low = (rest - middle.astype(jnp.float32)).astype(jnp.bfloat16)
    return high, middle, low


def whole(rows):
    rows = rows.astype(jnp.float32)
    lse = rows[:, :TILE] + rows[:, TILE : 2 * TILE] + rows[:, 2 * TILE :]
    return jnp.transpose(jnp.concatenate([lse] * (HD // 16), axis=0))


def attend_all(load, rel_tiles, refs, put):
    pattern_ref, reached_ref, kv_ref, ck_ref, cv_ref, bias_ref = refs
    parts, _, part, width = kv_ref.shape
    rows = parts * part
    fill_bias(bias_ref, pattern_ref, reached_ref, rel_tiles, rows // TILE, ck_ref.shape[0] // TILE)
    bias = [bias_ref[t, 0:1, :] for t in range(rows // TILE)]
    lane = lax.broadcasted_iota(jnp.int32, (rows, HD), 1)
    stats = jnp.zeros((rows, HD), jnp.float32)
    for h in range(width // HD):
        cols = slice(h * HD, (h + 1) * HD)
        k = kv_ref[:, 0, :, cols].reshape(rows, HD)
        v = kv_ref[:, 1, :, cols].reshape(rows, HD)
        out, lse = attend(load(cols), k, v, ck_ref[:, cols], cv_ref[:, cols], bias)
        put(cols, out)
        stats = jnp.where(lane == h, lse, stats)
    put(None, stats)


def put_partial(o_ref, rows, cols, value):
    if cols is not None:
        o_ref[:rows, cols] = value.astype(jnp.bfloat16)
        return
    for t in range(rows // TILE):
        for i, piece in enumerate(pieces(value[t * TILE : (t + 1) * TILE])):
            o_ref[rows:, (3 * t + i) * TILE : (3 * t + i + 1) * TILE] = piece


def far_kernel(
    pattern_ref, reached_ref, below_ref, above_ref, kv_ref, ck_ref, cv_ref, to_below_ref, to_above_ref, *scratch
):
    own = kv_ref.shape[0] * kv_ref.shape[2] // TILE
    refs = (pattern_ref, reached_ref, kv_ref, ck_ref, cv_ref, *scratch)
    at = lax.rem(lax.axis_index("ctx"), PLANE)
    sides = ((below_ref, to_below_ref, at > 0, -own), (above_ref, to_above_ref, at < PLANE - 1, own))
    for q_ref, o_ref, inside, base in sides:

        @pl.when(inside)
        def _(q_ref=q_ref, o_ref=o_ref, base=base):
            def load(cols):
                return q_ref[:, cols]

            put = functools.partial(put_partial, o_ref, own * TILE)
            attend_all(load, [base + t for t in range(own)], refs, put)


def jump_kernel(*args):
    pattern_ref, reached_ref, *given = args[:5]
    kv_ref, _, _ = args[5:8]
    taken, o_ref, refs = args[8:11], args[11], (pattern_ref, reached_ref, *args[5:8], *args[12:])
    own = kv_ref.shape[0] * kv_ref.shape[2] // TILE
    at = lax.rem(lax.axis_index("ctx"), PLANE)

    @pl.when(jnp.logical_or(at == 0, at == PLANE - 1))
    def _():
        base = jnp.where(at == 0, -own, own)

        def load(cols):
            return joined(given, slice(0, own * TILE), cols)

        put = functools.partial(put_partial, o_ref, own * TILE)
        attend_all(load, [base + t for t in range(own)], refs, put)
        first = 0
        for ref in taken:
            ref[...] = o_ref[first : first + ref.shape[0]]
            first += ref.shape[0]


def joined(refs, rows, cols):
    found, first = [], 0
    for ref in refs:
        low, high = max(rows.start - first, 0), min(rows.stop - first, ref.shape[0])
        if low < high:
            found.append(ref[low:high, cols])
        first += ref.shape[0]
    return found[0] if len(found) == 1 else jnp.concatenate(found, axis=0)


def own_kernel(pattern_ref, reached_ref, q_ref, kv_ref, ck_ref, cv_ref, o_ref, stats_ref, bias_ref):
    def put(cols, value):
        if cols is None:
            stats_ref[...] = value
        else:
            o_ref[:, cols] = value

    own = kv_ref.shape[0] * kv_ref.shape[2] // TILE
    refs = (pattern_ref, reached_ref, kv_ref, ck_ref, cv_ref, bias_ref)
    attend_all(lambda cols: q_ref[:, cols], list(range(own)), refs, put)


def mix_kernel(count, o_ref, stats_ref, low_ref, high_ref, part0_ref, part1_ref, part2_ref, gate_ref, out_ref):
    parts = (part0_ref, part1_ref, part2_ref)
    ctx = lax.axis_index("ctx")
    at = lax.rem(ctx, PLANE)
    first, last = at == 0, at == PLANE - 1
    head = lax.axis_index("head")
    rows, width = o_ref.shape
    heads = width // HD
    for t in range(rows // TILE):
        here = slice(t * TILE, (t + 1) * TILE)
        stat = slice(rows, rows + 16), slice(3 * t * TILE, 3 * (t + 1) * TILE)
        jumped = joined(parts, *stat)
        low = whole(jnp.where(first, jumped, low_ref[stat]))
        high = whole(jnp.where(last, jumped, high_ref[stat]))
        low = jnp.where(ctx > 0, low, NEGATIVE)
        high = jnp.where(ctx < count - 1, high, NEGATIVE)
        mine = stats_ref[here, :]
        peak = jnp.maximum(jnp.maximum(mine, low), high)
        mine, low, high = jnp.exp2(mine - peak), jnp.exp2(low - peak), jnp.exp2(high - peak)
        total = 1.0 / (mine + low + high)
        mine, low, high = mine * total, low * total, high * total
        for h in range(heads):
            cols = slice(h * HD, (h + 1) * HD)
            jumped = joined(parts, here, cols)
            gate = gate_ref[pl.ds(head * heads + h, 1), :]
            mixed = o_ref[here, cols] * mine[:, h : h + 1]
            mixed = mixed + jnp.where(first, jumped, low_ref[here, cols]).astype(jnp.float32) * low[:, h : h + 1]
            mixed = mixed + jnp.where(last, jumped, high_ref[here, cols]).astype(jnp.float32) * high[:, h : h + 1]
            out_ref[here, cols] = (mixed * gate).astype(jnp.bfloat16)


def attention_cost(tiles, rows, cached, width):
    pairs = tiles * TILE * (rows + cached)
    return pl.CostEstimate(
        flops=4 * pairs * width, bytes_accessed=4 * (rows + cached) * width, transcendentals=pairs * (width // HD)
    )


def local(queries, keys, values, cache_keys, cache_values, pattern, reached, gate):
    split = lax.axis_size("head")
    count = lax.axis_size("ctx")
    part, full = queries.shape
    width = full // split
    rows = part * split
    cached = cache_keys.shape[0]
    own = rows // TILE
    jumps = [(first - 1, first) for first in range(PLANE, count, PLANE)]
    corners = (PLANE - SIDE, SIDE - 1)
    up = [(i, i + 1) for i in range(count - 1) if (i + 1) % PLANE]
    down = [(b, a) for a, b in up]
    straight = jumps + [(b, a) for a, b in jumps]
    out, onward = [], []
    for rising, falling in (corners, corners[::-1]):
        ways = [(a, a + 1 - PLANE + rising, b) for a, b in jumps] + [(b, b + falling, a) for a, b in jumps]
        out.append([way[:2] for way in ways])
        onward.append([way[1:] for way in ways])

    def jump(x):
        return [shift(x[0], straight)] + [shift(shift(x[1 + i], out[i]), onward[i]) for i in range(2)]

    def shift(x, pairs):
        return lax.ppermute(x, "ctx", pairs)

    def blocks(x):
        return jnp.transpose(x.reshape(part, split, width), (1, 0, 2))

    q = lax.all_to_all(blocks(queries), "head", split_axis=0, concat_axis=0, tiled=True).reshape(rows, width)
    kv = jnp.stack([blocks(keys), blocks(values)], axis=1)
    q, kv = lax.optimization_barrier((q, kv))
    cuts = (rows - 2 * DETOUR, rows - DETOUR)
    jumped = jump([q[: cuts[0]], q[cuts[0] : cuts[1]], q[cuts[1] :]])
    from_below = shift(q, up)
    from_above = shift(q, down)
    kv = lax.all_to_all(kv, "head", split_axis=0, concat_axis=0, tiled=True)

    partial = rows + 16

    def shapes(*counts):
        return tuple(jax.ShapeDtypeStruct((n, width), jnp.bfloat16) for n in counts)

    bias = pltpu.VMEM((own, 8, rows + cached), jnp.float32)
    to_below, to_above = pl.pallas_call(
        far_kernel,
        out_shape=shapes(partial, partial),
        in_specs=[smem(), smem()] + [vmem()] * 5,
        out_specs=(vmem(),) * 2,
        scratch_shapes=[bias],
        cost_estimate=attention_cost(2 * own, rows, cached, width),
        compiler_params=pltpu.CompilerParams(vmem_limit_bytes=LIMIT),
        name="far",
    )(pattern, reached, from_below, from_above, kv, cache_keys, cache_values)
    got_high = shift(to_below, down)
    got_low = shift(to_above, up)
    jumped = pl.pallas_call(
        jump_kernel,
        out_shape=shapes(partial - 2 * DETOUR, DETOUR, DETOUR),
        in_specs=[smem(), smem()] + [vmem()] * 6,
        out_specs=(vmem(),) * 3,
        scratch_shapes=[pltpu.VMEM((partial, width), jnp.bfloat16), bias],
        cost_estimate=attention_cost(own, rows, cached, width),
        compiler_params=pltpu.CompilerParams(vmem_limit_bytes=LIMIT),
        name="jump",
    )(pattern, reached, *jumped, kv, cache_keys, cache_values)
    jumped = jump(jumped)
    mine, stats = pl.pallas_call(
        own_kernel,
        out_shape=(
            jax.ShapeDtypeStruct((rows, width), jnp.float32),
            jax.ShapeDtypeStruct((rows, HD), jnp.float32),
        ),
        in_specs=[smem(), smem()] + [vmem()] * 4,
        out_specs=(vmem(), vmem()),
        scratch_shapes=[bias],
        cost_estimate=attention_cost(own, rows, cached, width),
        compiler_params=pltpu.CompilerParams(vmem_limit_bytes=LIMIT),
        name="own",
    )(pattern, reached, q, kv, cache_keys, cache_values)
    out = pl.pallas_call(
        functools.partial(mix_kernel, count),
        out_shape=jax.ShapeDtypeStruct((rows, width), jnp.bfloat16),
        in_specs=[vmem()] * 8,
        out_specs=vmem(),
        compiler_params=pltpu.CompilerParams(vmem_limit_bytes=LIMIT),
        name="mix",
    )(mine, stats, got_low, got_high, *jumped, gate.reshape(full // HD, HD))
    out = lax.all_to_all(out.reshape(split, part, width), "head", split_axis=0, concat_axis=0, tiled=True)
    return jnp.transpose(out, (1, 0, 2)).reshape(part, full)


def solution(mesh):
    tokens = P(("ctx", "head"), None)
    cached = P("ctx", "head")
    return jax.shard_map(
        local,
        mesh=mesh,
        in_specs=(tokens, tokens, tokens, cached, cached, P(), P(), P()),
        out_specs=tokens,
        check_vma=False,
    )
```

```python
import functools
import math

import jax
import jax.numpy as jnp
from jax import lax
from jax.experimental import pallas as pl
from jax.experimental.pallas import tpu as pltpu
from jax.sharding import PartitionSpec as P


HD = 128
TILE = 128
REACH = 4
NEGATIVE = -1e30
LIMIT = 16 << 20
PLANE = 16
SIDE = 4
Q_DETOUR = 80
O_DETOUR = 48
LOG2E = math.log2(math.e)
NT = (((1,), (1,)), ((), ()))


def vmem():
    return pl.BlockSpec(memory_space=pltpu.VMEM)


def smem():
    return pl.BlockSpec(memory_space=pltpu.SMEM)


def tile_bias(pattern_ref, reached_ref, tile, cached_id, tile_count):
    row = jnp.clip(tile, 0, tile_count - 1)
    used = reached_ref[row]
    times = jnp.int32(0)
    for slot in range(REACH):
        hit = jnp.logical_and(slot < used, pattern_ref[REACH * row + slot] == cached_id)
        times = times + jnp.where(hit, 1, 0)
    bias = jnp.where(times == 1, 0.0, NEGATIVE)
    bias = jnp.where(times == 2, 1.0, bias)
    bias = jnp.where(times == 3, math.log2(3.0), bias)
    return jnp.where(times == 4, 2.0, bias)


def fill_bias(bias_ref, pattern_ref, reached_ref, rel_tiles, own_tiles, cached_tiles):
    ctx = lax.axis_index("ctx")
    tile_count = reached_ref.shape[0]
    for row, rel in enumerate(rel_tiles):
        for t in range(own_tiles):
            near = jnp.where(jnp.abs(rel - t) <= 2, 0.0, NEGATIVE)
            bias_ref[row, :, t * TILE : (t + 1) * TILE] = jnp.full((8, TILE), near, jnp.float32)
        for u in range(cached_tiles):
            bias = tile_bias(
                pattern_ref, reached_ref, ctx * own_tiles + rel, ctx * cached_tiles + u, tile_count
            )
            at = (own_tiles + u) * TILE
            bias_ref[row, :, at : at + TILE] = jnp.full((8, TILE), bias, jnp.float32)


def biased(scores, bias):
    scale = HD**-0.5 * LOG2E
    tiles = [scores[t * TILE : (t + 1) * TILE] * scale + row for t, row in enumerate(bias)]
    return jnp.concatenate(tiles, axis=0)


def attend(q, k, v, ck, cv, bias):
    near = lax.dot_general(q, k, NT, preferred_element_type=jnp.float32)
    far = lax.dot_general(q, ck, NT, preferred_element_type=jnp.float32)
    split = near.shape[1]
    near = biased(near, [row[:, :split] for row in bias])
    far = biased(far, [row[:, split:] for row in bias])
    peak = jnp.maximum(
        jnp.max(near, axis=1, keepdims=True), jnp.max(far, axis=1, keepdims=True)
    )
    near = jnp.exp2(near - peak)
    far = jnp.exp2(far - peak)
    total = jnp.sum(near, axis=1, keepdims=True) + jnp.sum(far, axis=1, keepdims=True)
    out = jnp.dot(near.astype(jnp.bfloat16), v, preferred_element_type=jnp.float32)
    out = out + jnp.dot(far.astype(jnp.bfloat16), cv, preferred_element_type=jnp.float32)
    return out / total, peak + jnp.log2(total)


def pieces(lse):
    lse = jnp.transpose(lse)[:16]
    high = lse.astype(jnp.bfloat16)
    rest = lse - high.astype(jnp.float32)
    middle = rest.astype(jnp.bfloat16)
    low = (rest - middle.astype(jnp.float32)).astype(jnp.bfloat16)
    return high, middle, low


def whole(rows):
    rows = rows.astype(jnp.float32)
    lse = rows[:, :TILE] + rows[:, TILE : 2 * TILE] + rows[:, 2 * TILE :]
    return jnp.transpose(jnp.concatenate([lse] * (HD // 16), axis=0))


def attend_all(load, rel_tiles, refs, put):
    pattern_ref, reached_ref, kv_ref, ck_ref, cv_ref, bias_ref = refs
    parts, _, part, width = kv_ref.shape
    rows = parts * part
    fill_bias(bias_ref, pattern_ref, reached_ref, rel_tiles, rows // TILE, ck_ref.shape[0] // TILE)
    bias = [bias_ref[t, 0:1, :] for t in range(rows // TILE)]
    lane = lax.broadcasted_iota(jnp.int32, (rows, HD), 1)
    stats = jnp.zeros((rows, HD), jnp.float32)
    for h in range(width // HD):
        cols = slice(h * HD, (h + 1) * HD)
        k = kv_ref[:, 0, :, cols].reshape(rows, HD)
        v = kv_ref[:, 1, :, cols].reshape(rows, HD)
        out, lse = attend(load(cols), k, v, ck_ref[:, cols], cv_ref[:, cols], bias)
        put(cols, out)
        stats = jnp.where(lane == h, lse, stats)
    put(None, stats)


def put_partial(o_ref, rows, cols, value):
    if cols is not None:
        o_ref[:rows, cols] = value.astype(jnp.bfloat16)
        return
    for t in range(rows // TILE):
        for i, piece in enumerate(pieces(value[t * TILE : (t + 1) * TILE])):
            o_ref[rows:, (3 * t + i) * TILE : (3 * t + i + 1) * TILE] = piece


def far_kernel(
    pattern_ref, reached_ref, below_ref, above_ref, kv_ref, ck_ref, cv_ref, to_below_ref, to_above_ref, *scratch
):
    own = kv_ref.shape[0] * kv_ref.shape[2] // TILE
    refs = (pattern_ref, reached_ref, kv_ref, ck_ref, cv_ref, *scratch)
    at = lax.rem(lax.axis_index("ctx"), PLANE)
    sides = ((below_ref, to_below_ref, at > 0, -own), (above_ref, to_above_ref, at < PLANE - 1, own))
    for q_ref, o_ref, inside, base in sides:

        @pl.when(inside)
        def _(q_ref=q_ref, o_ref=o_ref, base=base):
            def load(cols):
                return q_ref[:, cols]

            put = functools.partial(put_partial, o_ref, own * TILE)
            attend_all(load, [base + t for t in range(own)], refs, put)


def jump_kernel(*args):
    pattern_ref, reached_ref, *given = args[:5]
    kv_ref, _, _ = args[5:8]
    taken, o_ref, refs = args[8:11], args[11], (pattern_ref, reached_ref, *args[5:8], *args[12:])
    own = kv_ref.shape[0] * kv_ref.shape[2] // TILE
    at = lax.rem(lax.axis_index("ctx"), PLANE)

    @pl.when(jnp.logical_or(at == 0, at == PLANE - 1))
    def _():
        base = jnp.where(at == 0, -own, own)

        def load(cols):
            return joined(given, slice(0, own * TILE), cols)

        put = functools.partial(put_partial, o_ref, own * TILE)
        attend_all(load, [base + t for t in range(own)], refs, put)
        first = 0
        for ref in taken:
            ref[...] = o_ref[first : first + ref.shape[0]]
            first += ref.shape[0]


def joined(refs, rows, cols):
    found, first = [], 0
    for ref in refs:
        low, high = max(rows.start - first, 0), min(rows.stop - first, ref.shape[0])
        if low < high:
            found.append(ref[low:high, cols])
        first += ref.shape[0]
    return found[0] if len(found) == 1 else jnp.concatenate(found, axis=0)


def own_kernel(pattern_ref, reached_ref, q_ref, kv_ref, ck_ref, cv_ref, o_ref, stats_ref, bias_ref):
    def put(cols, value):
        if cols is None:
            stats_ref[...] = value
        else:
            o_ref[:, cols] = value

    own = kv_ref.shape[0] * kv_ref.shape[2] // TILE
    refs = (pattern_ref, reached_ref, kv_ref, ck_ref, cv_ref, bias_ref)
    attend_all(lambda cols: q_ref[:, cols], list(range(own)), refs, put)


def mix_kernel(count, o_ref, stats_ref, low_ref, high_ref, part0_ref, part1_ref, part2_ref, gate_ref, out_ref):
    parts = (part0_ref, part1_ref, part2_ref)
    ctx = lax.axis_index("ctx")
    at = lax.rem(ctx, PLANE)
    first, last = at == 0, at == PLANE - 1
    head = lax.axis_index("head")
    rows, width = o_ref.shape
    heads = width // HD
    for t in range(rows // TILE):
        here = slice(t * TILE, (t + 1) * TILE)
        stat = slice(rows, rows + 16), slice(3 * t * TILE, 3 * (t + 1) * TILE)
        jumped = joined(parts, *stat)
        low = whole(jnp.where(first, jumped, low_ref[stat]))
        high = whole(jnp.where(last, jumped, high_ref[stat]))
        low = jnp.where(ctx > 0, low, NEGATIVE)
        high = jnp.where(ctx < count - 1, high, NEGATIVE)
        mine = stats_ref[here, :]
        peak = jnp.maximum(jnp.maximum(mine, low), high)
        mine, low, high = jnp.exp2(mine - peak), jnp.exp2(low - peak), jnp.exp2(high - peak)
        total = 1.0 / (mine + low + high)
        mine, low, high = mine * total, low * total, high * total
        for h in range(heads):
            cols = slice(h * HD, (h + 1) * HD)
            jumped = joined(parts, here, cols)
            gate = gate_ref[pl.ds(head * heads + h, 1), :]
            mixed = o_ref[here, cols] * mine[:, h : h + 1]
            mixed = mixed + jnp.where(first, jumped, low_ref[here, cols]).astype(jnp.float32) * low[:, h : h + 1]
            mixed = mixed + jnp.where(last, jumped, high_ref[here, cols]).astype(jnp.float32) * high[:, h : h + 1]
            out_ref[here, cols] = (mixed * gate).astype(jnp.bfloat16)


def attention_cost(tiles, rows, cached, width):
    pairs = tiles * TILE * (rows + cached)
    return pl.CostEstimate(
        flops=4 * pairs * width, bytes_accessed=4 * (rows + cached) * width, transcendentals=pairs * (width // HD)
    )


def local(queries, keys, values, cache_keys, cache_values, pattern, reached, gate):
    split = lax.axis_size("head")
    count = lax.axis_size("ctx")
    part, full = queries.shape
    width = full // split
    rows = part * split
    cached = cache_keys.shape[0]
    own = rows // TILE
    jumps = [(first - 1, first) for first in range(PLANE, count, PLANE)]
    corners = (PLANE - SIDE, SIDE - 1)
    up = [(i, i + 1) for i in range(count - 1) if (i + 1) % PLANE]
    down = [(b, a) for a, b in up]
    straight = jumps + [(b, a) for a, b in jumps]
    out, onward = [], []
    for rising, falling in (corners, corners[::-1]):
        ways = [(a, a + 1 - PLANE + rising, b) for a, b in jumps] + [(b, b + falling, a) for a, b in jumps]
        out.append([way[:2] for way in ways])
        onward.append([way[1:] for way in ways])

    def jump(x):
        return [shift(x[0], straight)] + [shift(shift(x[1 + i], out[i]), onward[i]) for i in range(2)]

    def shift(x, pairs):
        return lax.ppermute(x, "ctx", pairs)

    pattern = pattern.reshape(pattern.size)

    def blocks(x):
        return jnp.transpose(x.reshape(part, split, width), (1, 0, 2))

    q = lax.all_to_all(blocks(queries), "head", split_axis=0, concat_axis=0, tiled=True).reshape(rows, width)
    kv = jnp.stack([blocks(keys), blocks(values)], axis=1)
    q, kv = lax.optimization_barrier((q, kv))
    cuts = (rows - 2 * Q_DETOUR, rows - Q_DETOUR)
    jumped = jump([q[: cuts[0]], q[cuts[0] : cuts[1]], q[cuts[1] :]])
    from_below = shift(q, up)
    from_above = shift(q, down)
    kv = lax.all_to_all(kv, "head", split_axis=0, concat_axis=0, tiled=True)

    partial = rows + 16

    def shapes(*counts):
        return tuple(jax.ShapeDtypeStruct((n, width), jnp.bfloat16) for n in counts)

    bias = pltpu.VMEM((own, 8, rows + cached), jnp.float32)
    to_below, to_above = pl.pallas_call(
        far_kernel,
        out_shape=shapes(partial, partial),
        in_specs=[smem(), smem()] + [vmem()] * 5,
        out_specs=(vmem(),) * 2,
        scratch_shapes=[bias],
        cost_estimate=attention_cost(2 * own, rows, cached, width),
        compiler_params=pltpu.CompilerParams(vmem_limit_bytes=LIMIT),
        name="far",
    )(pattern, reached, from_below, from_above, kv, cache_keys, cache_values)
    got_high = shift(to_below, down)
    got_low = shift(to_above, up)
    jumped = pl.pallas_call(
        jump_kernel,
        out_shape=shapes(partial - 2 * O_DETOUR, O_DETOUR, O_DETOUR),
        in_specs=[smem(), smem()] + [vmem()] * 6,
        out_specs=(vmem(),) * 3,
        scratch_shapes=[pltpu.VMEM((partial, width), jnp.bfloat16), bias],
        cost_estimate=attention_cost(own, rows, cached, width),
        compiler_params=pltpu.CompilerParams(vmem_limit_bytes=LIMIT),
        name="jump",
    )(pattern, reached, *jumped, kv, cache_keys, cache_values)
    jumped = jump(jumped)
    mine, stats = pl.pallas_call(
        own_kernel,
        out_shape=(
            jax.ShapeDtypeStruct((rows, width), jnp.float32),
            jax.ShapeDtypeStruct((rows, HD), jnp.float32),
        ),
        in_specs=[smem(), smem()] + [vmem()] * 4,
        out_specs=(vmem(), vmem()),
        scratch_shapes=[bias],
        cost_estimate=attention_cost(own, rows, cached, width),
        compiler_params=pltpu.CompilerParams(vmem_limit_bytes=LIMIT),
        name="own",
    )(pattern, reached, q, kv, cache_keys, cache_values)
    out = pl.pallas_call(
        functools.partial(mix_kernel, count),
        out_shape=jax.ShapeDtypeStruct((rows, width), jnp.bfloat16),
        in_specs=[vmem()] * 8,
        out_specs=vmem(),
        compiler_params=pltpu.CompilerParams(vmem_limit_bytes=LIMIT),
        name="mix",
    )(mine, stats, got_low, got_high, *jumped, gate.reshape(full // HD, HD))
    out = lax.all_to_all(out.reshape(split, part, width), "head", split_axis=0, concat_axis=0, tiled=True)
    return jnp.transpose(out, (1, 0, 2)).reshape(part, full)


def solution(mesh):
    tokens = P(("ctx", "head"), None)
    cached = P("ctx", "head")
    return jax.shard_map(
        local,
        mesh=mesh,
        in_specs=(tokens, tokens, tokens, cached, cached, P(), P(), P()),
        out_specs=tokens,
        check_vma=False,
    )
```
